32 devices in a mesh: rows: 8 (over z, y), cols: 4 (over x, core).
Axes of the slice: x: 2, y: 2, z: 4, core: 2. Of those that a mesh axis runs over, the one named last changes fastest.
Arguments:
- depth: float32 [128, 16384], P('rows', 'cols'), may hold values from 0.08 to 6.3, as said below
- hit_mask: int32 [128, 16384], P('rows', 'cols'), may hold values 0 or 1
- hit_count: int32 [128, 16384], P('rows', 'cols'), may hold values from 1 to 8
- grad_h: float32 [128, 16384], P('rows', 'cols'), may hold values from -6 to 6
- grad_v: float32 [128, 16384], P('rows', 'cols'), may hold values from -6 to 6
Outputs:
- solution_field: float32 [128, 16384], P('rows', 'cols')
- residual: float32 [128, 16384], P('rows', 'cols')
The draws below stay inside these ranges and needn't reach their ends.
Inputs may be any that keep to these rules, and one draw needn't show every extreme that they name: `depth`: positive depths.
All inputs are finite; a program needn't handle non-finite values. No bound on the sum of `hit_mask` on one device may be relied on, other than what follows from the above.
Results may differ from the reference program's by a relative error of at most 0.0003.
Values sent between devices are 32-bit elements; how exact they have to be, the bound alone decides.
A program may use at most 64 MiB of HBM per device.

```python
import math
import jax
import jax.numpy as jnp
from jax import lax

ITERS = 12
NR = 128
NC = 16384


def draw_depth(key, part):
    row = lax.broadcasted_iota(jnp.float32, (NR, NC), 0)
    column = lax.broadcasted_iota(jnp.float32, (NR, NC), 1)
    ramp = 0.3 * jnp.exp(math.log(10.0) * (0.5 * row / NR + 0.5 * column / NC))
    rough = jnp.exp(jax.random.uniform(key, (NR, NC), jnp.float32, -0.7, 0.7))
    return ramp * rough


def touch_ends(values, own_key, least, largest):
    longest = values.shape.index(max(values.shape))
    spots = []
    for shift in (0, 1):
        where = [jax.random.randint(jax.random.fold_in(own_key, axis), (), 0, length) for axis, length in enumerate(values.shape)]
        where[longest] = (where[longest] + shift) % values.shape[longest]
        spots.append(tuple(where))
    return values.at[spots[0]].set(least).at[spots[1]].set(largest)


def level_of(stream_key, dims, shards, low, top_value):
    factor_of, own = 1.0, jax.random.fold_in(stream_key, 6)
    for position, shards_of in shards:
        heights = jnp.exp(jax.random.uniform(jax.random.fold_in(own, position), (shards_of,), jnp.float32, low / len(shards), top_value / len(shards)))
        factor_of = factor_of * jnp.repeat(heights, dims[position] // shards_of).reshape([-1 if axis == position else 1 for axis in range(len(dims))])
    return factor_of


def noise(own_key, dims, width, bound, shards=(), held_as=jnp.bfloat16):
    level = level_of(own_key, dims, shards, -0.22, 0.18) if shards else 1.0
    result = jax.random.normal(own_key, dims, jnp.float32) * width * level
    return jnp.minimum(jnp.maximum(result, -bound), bound).astype(held_as)


def setup_inputs(seed: int = 0) -> dict:
    arg_keys = jax.random.split(jax.random.key(seed), 6)
    depth = draw_depth(jax.random.fold_in(arg_keys[5], 71), 0)
    hit_mask = touch_ends((jax.random.randint(arg_keys[1], (NR, NC), 0, 4) < 1).astype(jnp.int32), jax.random.fold_in(arg_keys[1], 1), 0, 1)
    hit_count = touch_ends(jax.random.randint(arg_keys[2], (NR, NC), 1, 9), jax.random.fold_in(arg_keys[2], 1), 1, 8).astype(jnp.int32)
    grad_h = noise(arg_keys[3], (NR, NC), 1.0, 6.0, ((0, 8), (1, 4)), jnp.float32)
    grad_v = noise(arg_keys[4], (NR, NC), 1.0, 6.0, ((0, 8), (1, 4)), jnp.float32)
    return dict(depth=depth, hit_mask=hit_mask, hit_count=hit_count, grad_h=grad_h, grad_v=grad_v)


prior_weight = 0.1
smooth_weight = 2.0


def build(depth, hit_mask, hit_count, grad_h, grad_v):
    column = lax.broadcasted_iota(jnp.int32, depth.shape, 1)
    row = lax.broadcasted_iota(jnp.int32, depth.shape, 0)
    east = jnp.where(column + 1 < NC, jnp.exp(-0.5 * grad_h * grad_h), 0.0)
    south = jnp.where(row + 1 < NR, jnp.exp(-0.5 * grad_v * grad_v), 0.0)
    west = jnp.pad(east, ((0, 0), (1, 0)))[:, :-1]
    north = jnp.pad(south, ((1, 0), (0, 0)))[:-1, :]
    confidence = (hit_mask * hit_count).astype(jnp.float32) + prior_weight
    center = confidence + smooth_weight * (east + west + south + north)
    return (center, east, west, south, north), confidence * depth


def operate(field, coefficients):
    center, east, west, south, north = coefficients
    padded = jnp.pad(field, 1)
    beside = east * padded[1:-1, 2:] + west * padded[1:-1, :-2] + south * padded[2:, 1:-1] + north * padded[:-2, 1:-1]
    return center * field - smooth_weight * beside


def reference(depth, hit_mask, hit_count, grad_h, grad_v):
    coefficients, right_side = build(depth, hit_mask, hit_count, grad_h, grad_v)
    solution_field = jnp.zeros_like(right_side)
    residual = right_side
    direction = right_side
    norm_now = jnp.sum(residual * residual)
    for iteration in range(ITERS):
        image = operate(direction, coefficients)
        alpha = norm_now / jnp.sum(direction * image)
        solution_field = solution_field + alpha * direction
        residual = residual - alpha * image
        norm_next = jnp.sum(residual * residual)
        direction = residual + (norm_next / norm_now) * direction
        norm_now = norm_next
    return solution_field, residual
```

```python
import functools

import jax
import jax.numpy as jnp
from jax import lax
from jax.experimental import pallas as pl
from jax.experimental.pallas import tpu as pltpu
from jax.sharding import PartitionSpec as P

ITERS = 12

prior_weight = 0.1
smooth_weight = 2.0
LANES = 128
SUB = 8
HALF = LANES // 2
MESH = pl.DeviceIdType.MESH

SCALE = 0.25
CENTER = 9.0 * SCALE
SPREAD = 16.0 * SCALE * SCALE
BLOCKS = (2, 2, 3, 3, 2)
KNOWN = 4
SWITCH = 7
DEPTH = max(BLOCKS)
GHOST = SUB
COPIES = 64


def each(start, stop, body):
    if stop - start < 32:
        for k in range(start, stop):
            body(k)
    else:
        lax.fori_loop(start, stop, lambda k, c: (body(k), c)[1], 0)


def factor(gram, size):
    s = {key: value for key, value in gram.items()}
    lower, pivots = {}, []
    for k in range(size):
        pivots.append(s[k, k])
        if k + 1 == size:
            break
        inverse = 1.0 / s[k, k]
        for i in range(k + 1, size):
            lower[i, k] = s[i, k] * inverse
        for i in range(k + 1, size):
            for j in range(k + 1, i + 1):
                if (i, j) in s:
                    s[i, j] = s[i, j] - lower[i, k] * s[j, k]
    return lower, pivots


def lanczos(gram, size, a):
    lower, pivots = factor(gram, size + 1)
    alphas = []
    for k in range(size):
        value = a[k] + lower[k + 1, k]
        alphas.append(value - lower[k, k - 1] if k else value)
    betas = [None] + [pivots[k] / pivots[k - 1] for k in range(1, len(pivots))]
    return alphas, betas


def added(x, y):
    return y if x is None else (x if y is None else x + y)


def times(c, x):
    return None if x is None or c is None else (x if isinstance(c, float) and c == 1.0 else c * x)


def minus(x, y):
    return x if y is None else (-y if x is None else x - y)


def applied(p, a, b, size):
    out = [None] * size
    for k, value in enumerate(p):
        if value is None:
            continue
        out[k] = added(out[k], times(a[k], value))
        if k + 1 < size:
            out[k + 1] = added(out[k + 1], value)
        if k:
            out[k - 1] = added(out[k - 1], times(b[k], value))
    return out


def kernel(
    nr, nc, rows, cols,
    depth, hit_mask, hit_count, grad_h, grad_v,
    x_out, r_out,
    basis, coef, strip, strip_coef, strip_next, strip_flow,
    edge_send, edge_left, edge_right, folds, by_device,
    send, recv, sum_send, sum_recv,
):
    me_r = lax.axis_index("rows")
    me_c = lax.axis_index("cols")
    J = cols // (SUB * LANES)
    tiles = cols // LANES
    R, D = rows, DEPTH
    bands = rows // SUB
    tall = rows + 2 * GHOST
    has_above, has_below = me_r > 0, me_r < nr - 1
    has_left, has_right = me_c > 0, me_c < nc - 1
    up, down = (me_r - 1, me_c), (me_r + 1, me_c)
    lefthand, righthand = (me_r, me_c - 1), (me_r, me_c + 1)
    devices = nr * nc
    me = me_r * nc + me_c

    def peer(k):
        other = lax.rem(me + k, devices)
        return (other // nc, lax.rem(other, nc))

    barrier = pltpu.get_barrier_semaphore()
    each(1, devices, lambda k: pl.semaphore_signal(barrier, inc=1, device_id=peer(k), device_id_type=MESH))

    sub_id = lax.broadcasted_iota(jnp.int32, (SUB, LANES), 0)
    lane_id = lax.broadcasted_iota(jnp.int32, (SUB, LANES), 1)
    zero = jnp.zeros((SUB, LANES), jnp.float32)

    used = [0]
    pending = []

    def copy(src, dst, to, sends, receives):
        k = used[0]
        used[0] += 1
        c = pltpu.make_async_remote_copy(
            src_ref=src, dst_ref=dst, send_sem=send.at[k], recv_sem=recv.at[k], device_id=to, device_id_type=MESH
        )
        pl.when(sends)(c.start)
        pending.append((c, sends))
        return c, receives

    def arrive(copies):
        for c, receives in copies:
            pl.when(receives)(c.wait_recv)

    def local(read, last_col, last_row):
        confidence = (read(hit_mask) * read(hit_count)).astype(jnp.float32) + prior_weight
        h, v = read(grad_h), read(grad_v)
        e = (SCALE * smooth_weight) * jnp.exp(-0.5 * h * h)
        s = (SCALE * smooth_weight) * jnp.exp(-0.5 * v * v)
        if last_col is not None:
            e = jnp.where(jnp.logical_and(last_col, jnp.logical_not(has_right)), 0.0, e)
        if last_row is not None:
            s = jnp.where(jnp.logical_and(last_row, jnp.logical_not(has_below)), 0.0, s)
        return SCALE * confidence, e, s, confidence * read(depth)

    for side in range(2):
        tile = (tiles - 1) * side
        for band in range(bands):
            start = (band * tiles + tile) * SUB
            values = local(
                lambda ref: ref[start : start + SUB, :],
                lane_id == LANES - 1 if side else None,
                sub_id == SUB - 1 if band == bands - 1 else None,
            )
            for n, value in enumerate(values):
                edge_send[side, band, n] = value

    def row_coefficients(r, last_row):
        band, within = r // SUB, lax.rem(r, SUB)
        for j in range(J):
            start = band * (tiles * SUB) + j * SUB + within
            c, e, s, b = local(
                lambda ref: ref[pl.ds(start, SUB, stride=J * SUB), :],
                jnp.logical_and(lane_id == LANES - 1, sub_id == SUB - 1) if j == J - 1 else None,
                sub_id >= 0 if last_row else None,
            )
            coef[0, D + r, j] = c
            coef[1, D + r, j] = e
            coef[2, D + r, j] = s
            basis[0, D + r, j] = b

    def coefficient_rows(start, stop, last=False):
        for r in range(start, stop):
            row_coefficients(r, last and r == R - 1)

    coefficient_rows(0, D)
    lax.fori_loop(0, (R - 2 * D) // 2, lambda i, c: ([row_coefficients(D + 2 * i + t, False) for t in range(2)], c)[1], 0)
    coefficient_rows(D + (R - 2 * D) // 2 * 2, R, True)

    def clear_ghost(first, strip_first):
        def _():
            for t in range(D):
                for j in range(J):
                    for n in range(3):
                        coef[n, first + t, j] = zero
                    for slot in exchanged:
                        basis[slot, first + t, j] = zero
            for side in range(2):
                for n in range(3):
                    strip_coef[n, side, strip_first : strip_first + GHOST, :] = zero
                for slot in strips_exchanged:
                    strip[slot, side, strip_first : strip_first + GHOST, :] = zero

        return _

    starts = [sum(BLOCKS[:n]) for n in range(len(BLOCKS))]

    def w_slot(k):
        return SWITCH + k if k else 0

    exchanged = sorted(
        {k if k < SWITCH else w_slot(k) for k in starts}
        | {(k - 1 if k < SWITCH else w_slot(k - 1)) for k in starts if k > 0}
        | set(range(SWITCH))
    )
    strips_exchanged = [0, w_slot(SWITCH - 1), w_slot(SWITCH)]
    pl.when(jnp.logical_not(has_above))(clear_ghost(0, 0))
    pl.when(jnp.logical_not(has_below))(clear_ghost(D + R, GHOST + R))

    @pl.when(jnp.logical_not(has_left))
    def _():
        edge_left[...] = jnp.zeros_like(edge_left)

    @pl.when(jnp.logical_not(has_right))
    def _():
        edge_right[...] = jnp.zeros_like(edge_right)

    pl.semaphore_wait(barrier, devices - 1)

    def send_rows(slot, first, count):
        if count <= 0:
            return []
        top = D + first - 1
        bottom = D + R - (first - 1) - count
        return [
            copy(basis.at[slot, pl.ds(top, count)], basis.at[slot, pl.ds(top + R, count)], up, has_above, has_below),
            copy(basis.at[slot, pl.ds(bottom, count)], basis.at[slot, pl.ds(bottom - R, count)], down, has_below, has_above),
        ]

    def send_coefs(old, new):
        copies = []
        count = new - old
        bottom = D + R - new
        copies.append(copy(coef.at[2, pl.ds(bottom, count)], coef.at[2, pl.ds(bottom - R, count)], down, has_below, has_above))
        low, high = max(old, 1), new - 1
        if high >= low:
            n = high - low + 1
            top = D + low - 1
            bottom = D + R - high
            copies.append(copy(coef.at[:, pl.ds(top, n)], coef.at[:, pl.ds(top + R, n)], up, has_above, has_below))
            copies.append(
                copy(coef.at[0:2, pl.ds(bottom, n)], coef.at[0:2, pl.ds(bottom - R, n)], down, has_below, has_above)
            )
        return copies

    def send_strips(slots):
        copies = []
        for slot in slots:
            copies.append(
                copy(
                    strip.at[slot, :, pl.ds(GHOST, GHOST)], strip.at[slot, :, pl.ds(GHOST + R, GHOST)],
                    up, has_above, has_below,
                )
            )
            copies.append(
                copy(strip.at[slot, :, pl.ds(R, GHOST)], strip.at[slot, :, pl.ds(0, GHOST)], down, has_below, has_above)
            )
        return copies

    def rolled(v, shift, axis):
        return pltpu.roll(v, shift % v.shape[axis], axis)

    def strip_ready(src):
        v = strip[src, 0]
        strip_flow[...] = rolled(strip_coef[1, 0] * (v - rolled(v, -1, 1)), 1, 1)
        strip_next[...] = rolled(strip[src, 1], -1, 1)

    def tall_wide(c):
        return c if isinstance(c, float) else jnp.concatenate([c] * (tall // SUB), axis=0)

    def strip_step(src, prev, dst, a, b):
        for side in range(2):
            v = strip[src, side]
            flow = strip_coef[1, side] * (v - rolled(v, -1, 1))
            fall = strip_coef[2, side] * (v - rolled(v, -1, 0))
            value = (strip_coef[0, side] - tall_wide(a)) * v + (flow - rolled(flow, 1, 1)) + (fall - rolled(fall, 1, 0))
            if b is not None:
                value = value - times(tall_wide(b), strip[prev, side])
            strip[dst, side] = value

    def step(src, prev, dst, a, b, reach):
        first, count = D - reach, R + 2 * reach
        unroll = next(u for u in (5, 6, 4, 3, 2, 1) if count % u == 0)

        def row(i, state):
            v, fall_above = state
            below = [basis[src, i + 1, j] for j in range(J)]
            fall = [coef[2, i, j] * (v[j] - below[j]) for j in range(J)]
            line = pl.ds(i + (GHOST - D), 1)
            to_left = [rolled(v[j], -1, 1) for j in range(J)]
            beyond = jnp.where(
                sub_id == SUB - 1, jnp.broadcast_to(strip_next[line, :], (SUB, LANES)), rolled(to_left[0], -1, 0)
            )
            flow = [
                coef[1, i, j] * (v[j] - jnp.where(lane_id == LANES - 1, to_left[j + 1] if j + 1 < J else beyond, to_left[j]))
                for j in range(J)
            ]
            to_right = [rolled(f, 1, 1) for f in flow]
            before = jnp.where(
                sub_id == 0, jnp.broadcast_to(strip_flow[line, :], (SUB, LANES)), rolled(to_right[J - 1], 1, 0)
            )
            for j in range(J):
                arriving = jnp.where(lane_id == 0, to_right[j - 1] if j else before, to_right[j])
                value = (coef[0, i, j] - a) * v[j] + ((flow[j] - arriving) + (fall[j] - fall_above[j]))
                if b is not None:
                    value = value - times(b, basis[prev, i, j])
                basis[dst, i, j] = value
            return below, fall

        def body(n, state):
            for t in range(unroll):
                state = row(first + n * unroll + t, state)
            return state

        v = [basis[src, first, j] for j in range(J)]
        fall = [coef[2, first - 1, j] * (basis[src, first - 1, j] - v[j]) for j in range(J)]
        lax.fori_loop(0, count // unroll, body, (v, fall))

    def advance(src, prev, dst, a, b, reach, more=True):
        strip_ready(src)
        step(src, prev, dst, a, b, reach)
        if more:
            strip_step(src, prev, dst, a, b)

    def dots(pairs, base):
        for g in range(0, len(pairs), 8):
            group = pairs[g : g + 8]
            slots = sorted({s for pair in group for s in pair})

            def body(i, sums):
                for j in range(J):
                    held = {s: basis[s, D + i, j] for s in slots}
                    sums = tuple(total + held[p] * held[q] for total, (p, q) in zip(sums, group))
                return sums

            sums = lax.fori_loop(0, R, body, (zero,) * len(group), unroll=2)
            for n, total in enumerate(sums):
                k = base + g + n
                folds[k : k + 1, :] = jnp.sum(total, axis=0, keepdims=True)

    def combine(targets, first, count):
        slots = sorted({s for _, terms in targets for s in terms})

        def body(i, c):
            for j in range(J):
                held = {s: basis[s, first + i, j] for s in slots}
                for target, terms in targets:
                    total = None
                    for s, weight in terms.items():
                        total = added(total, times(weight, held[s]))
                    if callable(target):
                        target(i, j, total)
                    else:
                        basis[target, first + i, j] = total
            return c

        lax.fori_loop(0, count, body, 0)

    def reduce(slot, count):
        n = -(-count // SUB) * SUB
        part = jnp.broadcast_to(jnp.sum(folds[0:n, :], axis=1, keepdims=True), (n, LANES))
        mine = lax.broadcasted_iota(jnp.int32, (n, LANES), 0) == lax.broadcasted_iota(jnp.int32, (n, LANES), 1)
        by_device[slot, me] = jnp.sum(jnp.where(mine, part, 0.0), axis=0, keepdims=True)

        def outgoing(k):
            here = by_device.at[slot, me]
            return pltpu.make_async_remote_copy(
                src_ref=here, dst_ref=here, send_sem=sum_send.at[slot, k], recv_sem=sum_recv.at[slot, me],
                device_id=peer(k), device_id_type=MESH,
            )

        each(1, devices, lambda k: outgoing(k).start())

        def finish():
            def arrival(k):
                source = lax.rem(me + k, devices)
                here = by_device.at[slot, source]
                pltpu.make_async_remote_copy(
                    src_ref=here, dst_ref=here, send_sem=sum_send.at[slot, k], recv_sem=sum_recv.at[slot, source],
                    device_id=peer(k), device_id_type=MESH,
                ).wait_recv()

            each(1, devices, arrival)
            each(1, devices, lambda k: outgoing(k).wait_send())
            if devices <= 32:
                parts = [by_device[slot, k] for k in range(devices)]
                while len(parts) > 1:
                    parts = [a + b for a, b in zip(parts[::2], parts[1::2])] + parts[len(parts) // 2 * 2 :]
                total = parts[0]
            else:
                total = lax.fori_loop(1, devices, lambda k, t: t + by_device[slot, k], by_device[slot, 0])
            return [jnp.broadcast_to(total[:, k : k + 1], (SUB, LANES)) for k in range(count)]

        return finish

    v_a = [CENTER] * SWITCH
    v_b = [None, 2.0 * SPREAD] + [SPREAD] * (SWITCH - 1)

    opening = send_rows(0, 1, BLOCKS[0]) + send_coefs(0, BLOCKS[0])
    sides = [
        copy(edge_send.at[0], edge_right, lefthand, has_left, has_right),
        copy(edge_send.at[1], edge_left, righthand, has_right, has_left),
    ]
    arrive(sides)
    for band in range(bands):
        own = slice(GHOST + band * SUB, GHOST + (band + 1) * SUB)
        for n in range(4):
            here = strip_coef.at[n] if n < 3 else strip.at[0]
            here[0, own, :] = jnp.where(lane_id < HALF, edge_send[0, band, n], edge_left[band, n])
            here[1, own, :] = jnp.where(lane_id < HALF, edge_right[band, n], edge_send[1, band, n])
    ghosts = send_strips([0]) + [
        copy(strip_coef.at[:, :, pl.ds(GHOST, GHOST)], strip_coef.at[:, :, pl.ds(GHOST + R, GHOST)], up, has_above, has_below),
        copy(strip_coef.at[:, :, pl.ds(R, GHOST)], strip_coef.at[:, :, pl.ds(0, GHOST)], down, has_below, has_above),
    ]
    deeper = []
    finish = None
    k = 0
    w_a = w_b = None
    for n, block in enumerate(BLOCKS):
        slot = (lambda i: i) if k < SWITCH else w_slot
        if n == 0:
            arrive(opening + ghosts)
        else:
            first = send_rows(slot(k), 1, block) + send_rows(slot(k - 1), 2, block - 2)
            if k == SWITCH:
                first = first + send_strips([slot(k - 1), slot(k)])
            if n == 1 and BLOCKS[0] < D:
                deeper = send_coefs(BLOCKS[0], D)
            if k == KNOWN:
                pairs = [(i, j) for i in range(KNOWN + 1) for j in range(i + 1)]
                dots(pairs, 0)
                finish = reduce(0, len(pairs))
            if k == SWITCH:
                combine([(w_slot(i), {s: weights[i][s] for s in range(i + 1)}) for i in range(1, SWITCH - 1)], D, R)
                grams = [(i, j) for i in range(SWITCH + 1) for j in range(i + 1)]
                dots([(w_slot(i), w_slot(j)) for i, j in grams], 0)
            elif k > SWITCH:
                more = [(i, j) for i in range(starts[n - 1] + 1, k + 1) for j in range(i + 1)]
                dots([(w_slot(i), w_slot(j)) for i, j in more], len(grams))
                grams = grams + more
            arrive(first)
            if block == D and deeper:
                arrive(deeper)
                deeper = []
        for t in range(block):
            a = v_a[k] if k < SWITCH else w_a[k]
            b = v_b[k] if k < SWITCH else w_b[k]
            advance(slot(k), slot(k - 1) if k else None, slot(k + 1), a, b, block - 1 - t, k + 1 < ITERS)
            k += 1
        if k == SWITCH:
            totals = finish()
            gram = {pair: total for pair, total in zip(pairs, totals)}
            alphas, betas = lanczos(gram, KNOWN, v_a)
            w_a = alphas + [alphas[-1]] * (ITERS - KNOWN)
            w_b = betas + [betas[-1]] * (ITERS - KNOWN)
            one = jnp.ones((SUB, LANES), jnp.float32)
            weights = [[one]]
            for i in range(SWITCH):
                value = applied(weights[i] + [None], v_a + [None], v_b + [None], i + 2)
                value = [minus(p, times(w_a[i], q)) for p, q in zip(value, weights[i] + [None])]
                if i:
                    value = [minus(p, times(w_b[i], q)) for p, q in zip(value, weights[i - 1] + [None] * 2)]
                weights.append(value)
            final = [(w_slot(i), {s: weights[i][s] for s in range(i + 1)}) for i in (SWITCH - 1, SWITCH)]
            combine(final, D, R)
            combine(final[:1], D - 1, 1)
            combine(final[:1], D + R, 1)
            for target, terms in final:
                for side in range(2):
                    for band in range(bands):
                        own = slice(GHOST + band * SUB, GHOST + (band + 1) * SUB)
                        total = None
                        for s, weight in terms.items():
                            total = added(total, times(weight, strip[s, side, own, :]))
                        strip[target, side, own, :] = total

    more = [(i, j) for i in range(starts[-1] + 1, ITERS + 1) for j in range(i + 1) if j < ITERS]
    dots([(w_slot(i), w_slot(j)) for i, j in more], len(grams))
    grams = grams + more
    totals = reduce(1, len(grams))()
    gram = {pair: total for pair, total in zip(grams, totals)}
    gram[ITERS, ITERS] = zero
    alphas, betas = lanczos(gram, ITERS, w_a)
    one = jnp.ones((SUB, LANES), jnp.float32)
    x, r, p = [None] * (ITERS + 1), [one], [one]
    w_a = w_a + [None]
    w_b = w_b + [None]
    inverse = None
    for i in range(ITERS):
        pivot = alphas[i] if i == 0 else alphas[i] - betas[i] * inverse
        inverse = 1.0 / pivot
        image = applied(p + [None], w_a, w_b, i + 2)
        gain = SCALE * inverse
        x = [added(q, times(gain, s)) for q, s in zip(x, p + [None] * (ITERS + 1 - len(p)))]
        r = [minus(q, times(inverse, s)) for q, s in zip(r + [None], image)]
        if i + 1 < ITERS:
            ratio = betas[i + 1] * inverse * inverse
            p = [added(q, times(ratio, s)) for q, s in zip(r, p + [None])]

    def store(ref):
        def put(i, j, value):
            band, within = i // SUB, lax.rem(i, SUB)
            ref[pl.ds(band * (tiles * SUB) + j * SUB + within, SUB, stride=J * SUB), :] = value

        return put

    combine(
        [
            (store(x_out), {w_slot(i): x[i] for i in range(ITERS)}),
            (store(r_out), {w_slot(i): r[i] for i in range(ITERS + 1)}),
        ],
        D, R,
    )
    for c, sends in pending:
        pl.when(sends)(c.wait_send)


def solution(mesh):
    nr, nc = mesh.shape["rows"], mesh.shape["cols"]

    def on_device(*inputs):
        rows, cols = inputs[0].shape
        bands, tiles, chunk = rows // SUB, cols // LANES, cols // (SUB * LANES)

        def pieces(a):
            return a.reshape(bands, SUB, tiles, LANES).transpose(0, 2, 1, 3).reshape(bands * tiles * SUB, LANES)

        def whole(a):
            return a.reshape(bands, tiles, SUB, LANES).transpose(0, 2, 1, 3).reshape(rows, cols)

        def held(*shape):
            return pltpu.VMEM(shape, jnp.float32)

        block = jax.ShapeDtypeStruct((bands * tiles * SUB, LANES), jnp.float32)
        high, tall = rows + 2 * DEPTH, rows + 2 * GHOST
        slots = SWITCH + ITERS + 1
        dma = pltpu.SemaphoreType.DMA
        x, r = pl.pallas_call(
            functools.partial(kernel, nr, nc, rows, cols),
            out_shape=(block, block),
            in_specs=[pl.BlockSpec(memory_space=pltpu.VMEM)] * 5,
            out_specs=[pl.BlockSpec(memory_space=pltpu.VMEM)] * 2,
            scratch_shapes=[
                held(slots, high, chunk, SUB, LANES),
                held(3, high, chunk, SUB, LANES),
                held(slots, 2, tall, LANES),
                held(3, 2, tall, LANES),
                held(tall, LANES),
                held(tall, LANES),
                held(2, bands, 4, SUB, LANES),
                held(bands, 4, SUB, LANES),
                held(bands, 4, SUB, LANES),
                held(96, LANES),
                held(2, nr * nc, 1, LANES),
                dma((COPIES,)), dma((COPIES,)), dma((2, nr * nc)), dma((2, nr * nc)),
            ],
            compiler_params=pltpu.CompilerParams(collective_id=0, has_side_effects=True),
        )(*(pieces(a) for a in inputs))
        return whole(x), whole(r)

    spec = P("rows", "cols")
    return jax.shard_map(
        on_device, mesh=mesh, in_specs=(spec,) * 5, out_specs=(spec, spec), check_vma=False
    )
```

```python
import functools

import jax
import jax.numpy as jnp
from jax import lax
from jax.experimental import pallas as pl
from jax.experimental.pallas import tpu as pltpu
from jax.sharding import PartitionSpec as P

ITERS = 12

prior_weight = 0.1
smooth_weight = 2.0
LANES = 128
SUB = 8
HALF = LANES // 2
MESH = pl.DeviceIdType.MESH

SCALE = 0.25
CENTER = 9.0 * SCALE
SPREAD = 16.0 * SCALE * SCALE
BLOCKS = (2, 2, 3, 3, 2)
KNOWN = 4
SWITCH = 7
DEPTH = max(BLOCKS)
GHOST = SUB
COPIES = 64


def each(start, stop, body):
    if stop - start < 32:
        for k in range(start, stop):
            body(k)
    else:
        lax.fori_loop(start, stop, lambda k, c: (body(k), c)[1], 0)


class Lanczos:
    def __init__(self, a):
        self.a, self.lower, self.pivots, self.inverses = a, {}, [], []
        self.alphas, self.betas = [], [None]

    def row(self, k, entries, last=False):
        reduced = []
        for j in range(k):
            value = entries[j]
            for i in range(j):
                value = value - reduced[i] * self.lower[j, i]
            reduced.append(value)
            self.lower[k, j] = value * self.inverses[j]
        if k:
            value = self.a[k - 1] + self.lower[k, k - 1]
            self.alphas.append(value - self.lower[k - 1, k - 2] if k > 1 else value)
        if last:
            return
        pivot = entries[k]
        for i in range(k):
            pivot = pivot - reduced[i] * self.lower[k, i]
        if k:
            self.betas.append(pivot * self.inverses[-1])
        self.pivots.append(pivot)
        self.inverses.append(1.0 / pivot)


def added(x, y):
    return y if x is None else (x if y is None else x + y)


def times(c, x):
    return None if x is None or c is None else (x if isinstance(c, float) and c == 1.0 else c * x)


def minus(x, y):
    return x if y is None else (-y if x is None else x - y)


def applied(p, a, b, size):
    out = [None] * size
    for k, value in enumerate(p):
        if value is None:
            continue
        out[k] = added(out[k], times(a[k], value))
        if k + 1 < size:
            out[k + 1] = added(out[k + 1], value)
        if k:
            out[k - 1] = added(out[k - 1], times(b[k], value))
    return out


def kernel(
    nr, nc, rows, cols,
    depth, hit_mask, hit_count, grad_h, grad_v,
    x_out, r_out,
    basis, coef, strip, strip_coef, strip_next, strip_flow,
    edge_send, edge_left, edge_right, folds, by_device,
    send, recv, sum_send, sum_recv,
):
    me_r = lax.axis_index("rows")
    me_c = lax.axis_index("cols")
    J = cols // (SUB * LANES)
    tiles = cols // LANES
    R, D = rows, DEPTH
    bands = rows // SUB
    tall = rows + 2 * GHOST
    has_above, has_below = me_r > 0, me_r < nr - 1
    has_left, has_right = me_c > 0, me_c < nc - 1
    up, down = (me_r - 1, me_c), (me_r + 1, me_c)
    lefthand, righthand = (me_r, me_c - 1), (me_r, me_c + 1)
    devices = nr * nc
    me = me_r * nc + me_c

    def peer(k):
        other = lax.rem(me + k, devices)
        return (other // nc, lax.rem(other, nc))

    barrier = pltpu.get_barrier_semaphore()
    each(1, devices, lambda k: pl.semaphore_signal(barrier, inc=1, device_id=peer(k), device_id_type=MESH))

    sub_id = lax.broadcasted_iota(jnp.int32, (SUB, LANES), 0)
    lane_id = lax.broadcasted_iota(jnp.int32, (SUB, LANES), 1)
    zero = jnp.zeros((SUB, LANES), jnp.float32)

    used = [0]
    pending = []

    def copy(src, dst, to, sends, receives):
        k = used[0]
        used[0] += 1
        c = pltpu.make_async_remote_copy(
            src_ref=src, dst_ref=dst, send_sem=send.at[k], recv_sem=recv.at[k], device_id=to, device_id_type=MESH
        )
        pl.when(sends)(c.start)
        pending.append((c, sends))
        return c, receives

    def arrive(copies):
        for c, receives in copies:
            pl.when(receives)(c.wait_recv)

    def local(read, last_col, last_row):
        confidence = (read(hit_mask) * read(hit_count)).astype(jnp.float32) + prior_weight
        h, v = read(grad_h), read(grad_v)
        e = (SCALE * smooth_weight) * jnp.exp(-0.5 * h * h)
        s = (SCALE * smooth_weight) * jnp.exp(-0.5 * v * v)
        if last_col is not None:
            e = jnp.where(jnp.logical_and(last_col, jnp.logical_not(has_right)), 0.0, e)
        if last_row is not None:
            s = jnp.where(jnp.logical_and(last_row, jnp.logical_not(has_below)), 0.0, s)
        return SCALE * confidence, e, s, confidence * read(depth)

    for side in range(2):
        tile = (tiles - 1) * side
        for band in range(bands):
            start = (band * tiles + tile) * SUB
            values = local(
                lambda ref: ref[start : start + SUB, :],
                lane_id == LANES - 1 if side else None,
                sub_id == SUB - 1 if band == bands - 1 else None,
            )
            for n, value in enumerate(values):
                edge_send[side, band, n] = value

    def row_coefficients(r, last_row):
        band, within = r // SUB, lax.rem(r, SUB)
        for j in range(J):
            start = band * (tiles * SUB) + j * SUB + within
            c, e, s, b = local(
                lambda ref: ref[pl.ds(start, SUB, stride=J * SUB), :],
                jnp.logical_and(lane_id == LANES - 1, sub_id == SUB - 1) if j == J - 1 else None,
                sub_id >= 0 if last_row else None,
            )
            coef[0, D + r, j] = c
            coef[1, D + r, j] = e
            coef[2, D + r, j] = s
            basis[0, D + r, j] = b

    def coefficient_rows(start, stop, last=False):
        for r in range(start, stop):
            row_coefficients(r, last and r == R - 1)

    coefficient_rows(0, D)
    lax.fori_loop(0, (R - 2 * D) // 2, lambda i, c: ([row_coefficients(D + 2 * i + t, False) for t in range(2)], c)[1], 0)
    coefficient_rows(D + (R - 2 * D) // 2 * 2, R, True)

    def clear_ghost(first, strip_first):
        def _():
            for t in range(D):
                for j in range(J):
                    for n in range(3):
                        coef[n, first + t, j] = zero
                    for slot in exchanged:
                        basis[slot, first + t, j] = zero
            for side in range(2):
                for n in range(3):
                    strip_coef[n, side, strip_first : strip_first + GHOST, :] = zero
                for slot in strips_exchanged:
                    strip[slot, side, strip_first : strip_first + GHOST, :] = zero

        return _

    starts = [sum(BLOCKS[:n]) for n in range(len(BLOCKS))]

    def w_slot(k):
        return SWITCH + k if k else 0

    exchanged = sorted(
        {k if k < SWITCH else w_slot(k) for k in starts}
        | {(k - 1 if k < SWITCH else w_slot(k - 1)) for k in starts if k > 0}
        | set(range(SWITCH))
    )
    strips_exchanged = [0, w_slot(SWITCH - 1), w_slot(SWITCH)]
    pl.when(jnp.logical_not(has_above))(clear_ghost(0, 0))
    pl.when(jnp.logical_not(has_below))(clear_ghost(D + R, GHOST + R))

    @pl.when(jnp.logical_not(has_left))
    def _():
        edge_left[...] = jnp.zeros_like(edge_left)

    @pl.when(jnp.logical_not(has_right))
    def _():
        edge_right[...] = jnp.zeros_like(edge_right)

    pl.semaphore_wait(barrier, devices - 1)

    def send_rows(slot, first, count):
        if count <= 0:
            return []
        top = D + first - 1
        bottom = D + R - (first - 1) - count
        return [
            copy(basis.at[slot, pl.ds(top, count)], basis.at[slot, pl.ds(top + R, count)], up, has_above, has_below),
            copy(basis.at[slot, pl.ds(bottom, count)], basis.at[slot, pl.ds(bottom - R, count)], down, has_below, has_above),
        ]

    def send_coefs(old, new):
        copies = []
        count = new - old
        bottom = D + R - new
        copies.append(copy(coef.at[2, pl.ds(bottom, count)], coef.at[2, pl.ds(bottom - R, count)], down, has_below, has_above))
        low, high = max(old, 1), new - 1
        if high >= low:
            n = high - low + 1
            top = D + low - 1
            bottom = D + R - high
            copies.append(copy(coef.at[:, pl.ds(top, n)], coef.at[:, pl.ds(top + R, n)], up, has_above, has_below))
            copies.append(
                copy(coef.at[0:2, pl.ds(bottom, n)], coef.at[0:2, pl.ds(bottom - R, n)], down, has_below, has_above)
            )
        return copies

    def send_strips(slots):
        copies = []
        for slot in slots:
            copies.append(
                copy(
                    strip.at[slot, :, pl.ds(GHOST, GHOST)], strip.at[slot, :, pl.ds(GHOST + R, GHOST)],
                    up, has_above, has_below,
                )
            )
            copies.append(
                copy(strip.at[slot, :, pl.ds(R, GHOST)], strip.at[slot, :, pl.ds(0, GHOST)], down, has_below, has_above)
            )
        return copies

    def rolled(v, shift, axis):
        return pltpu.roll(v, shift % v.shape[axis], axis)

    everywhere, inside = slice(0, tall), slice(GHOST, GHOST + R)

    def strip_ready(src, t, lines):
        v = strip[src, 0, lines, :]
        strip_flow[t, lines, :] = rolled(strip_coef[1, 0, lines, :] * (v - rolled(v, -1, 1)), 1, 1)
        strip_next[t, lines, :] = rolled(strip[src, 1, lines, :], -1, 1)

    def strip_step(src, prev, dst, a, b, lines):
        def spread(c):
            return c if isinstance(c, float) else jnp.concatenate([c] * ((lines.stop - lines.start) // SUB), axis=0)

        for side in range(2):
            v = strip[src, side, lines, :]
            flow = strip_coef[1, side, lines, :] * (v - rolled(v, -1, 1))
            fall = strip_coef[2, side, lines, :] * (v - rolled(v, -1, 0))
            value = (strip_coef[0, side, lines, :] - spread(a)) * v
            value = value + (flow - rolled(flow, 1, 1)) + (fall - rolled(fall, 1, 0))
            if b is not None:
                value = value - times(spread(b), strip[prev, side, lines, :])
            strip[dst, side, lines, :] = value

    def step(src, prev, dst, a, b, t, first, count, loop):
        def row(i, state):
            v, fall_above = state
            below = [basis[src, i + 1, j] for j in range(J)]
            fall = [coef[2, i, j] * (v[j] - below[j]) for j in range(J)]
            line = pl.ds(i + (GHOST - D), 1)
            to_left = [rolled(v[j], -1, 1) for j in range(J)]
            beyond = jnp.where(
                sub_id == SUB - 1, jnp.broadcast_to(strip_next[t, line, :], (SUB, LANES)), rolled(to_left[0], -1, 0)
            )
            flow = [
                coef[1, i, j] * (v[j] - jnp.where(lane_id == LANES - 1, to_left[j + 1] if j + 1 < J else beyond, to_left[j]))
                for j in range(J)
            ]
            to_right = [rolled(f, 1, 1) for f in flow]
            before = jnp.where(
                sub_id == 0, jnp.broadcast_to(strip_flow[t, line, :], (SUB, LANES)), rolled(to_right[J - 1], 1, 0)
            )
            for j in range(J):
                arriving = jnp.where(lane_id == 0, to_right[j - 1] if j else before, to_right[j])
                value = (coef[0, i, j] - a) * v[j] + ((flow[j] - arriving) + (fall[j] - fall_above[j]))
                if b is not None:
                    value = value - times(b, basis[prev, i, j])
                basis[dst, i, j] = value
            return below, fall

        v = [basis[src, first, j] for j in range(J)]
        state = v, [coef[2, first - 1, j] * (basis[src, first - 1, j] - v[j]) for j in range(J)]
        if not loop:
            for i in range(first, first + count):
                state = row(i, state)
            return
        unroll = next(u for u in (7, 6, 5, 4, 3, 2, 1) if count % u == 0)

        def body(n, state):
            for m in range(unroll):
                state = row(first + n * unroll + m, state)
            return state

        lax.fori_loop(0, count // unroll, body, state)

    def inner(recurrence, more, again):
        lines = inside if again else everywhere
        for t, (src, prev, dst, a, b) in enumerate(recurrence):
            strip_ready(src, t, lines)
            step(src, prev, dst, a, b, t, D + t + 1, R - 2 - 2 * t, True)
            if more or t + 1 < len(recurrence):
                strip_step(src, prev, dst, a, b, lines)

    def outer(recurrence, more, again):
        depth = len(recurrence)
        for t, (src, prev, dst, a, b) in enumerate(recurrence):
            if again:
                strip_ready(src, t, everywhere)
            step(src, prev, dst, a, b, t, D - (depth - 1 - t), depth, False)
            step(src, prev, dst, a, b, t, D + R - 1 - t, depth, False)
            if again and (more or t + 1 < depth):
                strip_step(src, prev, dst, a, b, everywhere)

    def dots(pairs, base):
        for g in range(0, len(pairs), 8):
            group = pairs[g : g + 8]
            slots = sorted({s for pair in group for s in pair})

            def body(i, sums):
                for j in range(J):
                    held = {s: basis[s, D + i, j] for s in slots}
                    sums = tuple(total + held[p] * held[q] for total, (p, q) in zip(sums, group))
                return sums

            sums = lax.fori_loop(0, R, body, (zero,) * len(group), unroll=2)
            for n, total in enumerate(sums):
                k = base + g + n
                folds[k : k + 1, :] = jnp.sum(total, axis=0, keepdims=True)

    def combine(targets, first, count):
        slots = sorted({s for _, terms in targets for s in terms})

        def body(i, c):
            for j in range(J):
                held = {s: basis[s, first + i, j] for s in slots}
                for target, terms in targets:
                    total = None
                    for s, weight in terms.items():
                        total = added(total, times(weight, held[s]))
                    if callable(target):
                        target(i, j, total)
                    else:
                        basis[target, first + i, j] = total
            return c

        lax.fori_loop(0, count, body, 0)

    def reduce(slot, count):
        n = -(-count // SUB) * SUB
        part = jnp.broadcast_to(jnp.sum(folds[0:n, :], axis=1, keepdims=True), (n, LANES))
        mine = lax.broadcasted_iota(jnp.int32, (n, LANES), 0) == lax.broadcasted_iota(jnp.int32, (n, LANES), 1)
        by_device[slot, me] = jnp.sum(jnp.where(mine, part, 0.0), axis=0, keepdims=True)

        def outgoing(k):
            here = by_device.at[slot, me]
            return pltpu.make_async_remote_copy(
                src_ref=here, dst_ref=here, send_sem=sum_send.at[slot, k], recv_sem=sum_recv.at[slot, me],
                device_id=peer(k), device_id_type=MESH,
            )

        each(1, devices, lambda k: outgoing(k).start())

        def finish():
            def arrival(k):
                source = lax.rem(me + k, devices)
                here = by_device.at[slot, source]
                pltpu.make_async_remote_copy(
                    src_ref=here, dst_ref=here, send_sem=sum_send.at[slot, k], recv_sem=sum_recv.at[slot, source],
                    device_id=peer(k), device_id_type=MESH,
                ).wait_recv()

            each(1, devices, arrival)
            each(1, devices, lambda k: outgoing(k).wait_send())
            if devices <= 32:
                parts = [by_device[slot, k] for k in range(devices)]
                while len(parts) > 1:
                    parts = [a + b for a, b in zip(parts[::2], parts[1::2])] + parts[len(parts) // 2 * 2 :]
                total = parts[0]
            else:
                total = lax.fori_loop(1, devices, lambda k, t: t + by_device[slot, k], by_device[slot, 0])
            return [jnp.broadcast_to(total[:, k : k + 1], (SUB, LANES)) for k in range(count)]

        return finish

    v_a = [CENTER] * SWITCH
    v_b = [None, 2.0 * SPREAD] + [SPREAD] * (SWITCH - 1)

    opening = send_rows(0, 1, BLOCKS[0]) + send_coefs(0, BLOCKS[0])
    sides = [
        copy(edge_send.at[0], edge_right, lefthand, has_left, has_right),
        copy(edge_send.at[1], edge_left, righthand, has_right, has_left),
    ]
    arrive(sides)
    for band in range(bands):
        own = slice(GHOST + band * SUB, GHOST + (band + 1) * SUB)
        for n in range(4):
            here = strip_coef.at[n] if n < 3 else strip.at[0]
            here[0, own, :] = jnp.where(lane_id < HALF, edge_send[0, band, n], edge_left[band, n])
            here[1, own, :] = jnp.where(lane_id < HALF, edge_right[band, n], edge_send[1, band, n])
    ghosts = send_strips([0]) + [
        copy(strip_coef.at[:, :, pl.ds(GHOST, GHOST)], strip_coef.at[:, :, pl.ds(GHOST + R, GHOST)], up, has_above, has_below),
        copy(strip_coef.at[:, :, pl.ds(R, GHOST)], strip_coef.at[:, :, pl.ds(0, GHOST)], down, has_below, has_above),
    ]
    deeper = []
    k = 0
    w_a = w_b = None
    one = jnp.ones((SUB, LANES), jnp.float32)
    for n, block in enumerate(BLOCKS):
        slot = (lambda i: i) if k < SWITCH else w_slot
        more = k + block < ITERS
        if n == 0:
            copies = opening + ghosts
        else:
            copies = send_rows(slot(k), 1, block) + send_rows(slot(k - 1), 2, block - 2)
            if k == SWITCH:
                copies = copies + send_strips([slot(k - 1), slot(k)])
            if n == 1 and BLOCKS[0] < D:
                deeper = send_coefs(BLOCKS[0], D)
        v_or_w = (v_a, v_b) if k < SWITCH else (w_a, w_b)
        recurrence = [
            (slot(i), slot(i - 1) if i else None, slot(i + 1), v_or_w[0][i], v_or_w[1][i]) for i in range(k, k + block)
        ]
        if k == KNOWN:
            pairs = [(i, j) for i in range(KNOWN + 1) for j in range(i + 1)]
            dots(pairs, 0)
            early = reduce(0, len(pairs))
        if k == SWITCH:
            combine(final, D + D, R - 2 * D)
        again = n == 0 or k == SWITCH
        inner(recurrence, more, again)
        if k == SWITCH:
            combine([(w_slot(i), {s: weights[i][s] for s in range(i + 1)}) for i in range(1, SWITCH - 1)], D, R)
            grams = [(i, j) for i in range(SWITCH + 1) for j in range(i + 1)]
            dots([(w_slot(i), w_slot(j)) for i, j in grams], 0)
        elif k > SWITCH:
            added_pairs = [(i, j) for i in range(starts[n - 1] + 1, k + 1) for j in range(i + 1)]
            dots([(w_slot(i), w_slot(j)) for i, j in added_pairs], len(grams))
            grams = grams + added_pairs
            if not more:
                middle = reduce(1, len(grams))
        arrive(copies)
        if block == D and deeper:
            arrive(deeper)
            deeper = []
        outer(recurrence, more, again)
        k += block
        if k == SWITCH:
            entries = dict(zip(pairs, early()))
            known = Lanczos(v_a)
            for i in range(KNOWN + 1):
                known.row(i, [entries[i, j] for j in range(i + 1)])
            w_a = known.alphas + [known.alphas[-1]] * (ITERS - KNOWN)
            w_b = known.betas + [known.betas[-1]] * (ITERS - KNOWN)
            weights = [[one]]
            for i in range(SWITCH):
                value = applied(weights[i] + [None], v_a + [None], v_b + [None], i + 2)
                value = [minus(p, times(w_a[i], q)) for p, q in zip(value, weights[i] + [None])]
                if i:
                    value = [minus(p, times(w_b[i], q)) for p, q in zip(value, weights[i - 1] + [None] * 2)]
                weights.append(value)
            final = [(w_slot(i), {s: weights[i][s] for s in range(i + 1)}) for i in (SWITCH - 1, SWITCH)]
            combine(final[:1], D - 1, 1)
            combine(final[:1], D + R, 1)
            combine(final, D, D)
            combine(final, D + R - D, D)
            for target, terms in final:
                for side in range(2):
                    for band in range(bands):
                        own = slice(GHOST + band * SUB, GHOST + (band + 1) * SUB)
                        total = None
                        for s, weight in terms.items():
                            total = added(total, times(weight, strip[s, side, own, :]))
                        strip[target, side, own, :] = total

    full = starts[-1]
    direct = [(i, j) for i in range(full + 1, ITERS + 1) for j in (i - 1, i) if j < ITERS]
    dots([(w_slot(i), w_slot(j)) for i, j in direct], 0)
    late = reduce(2, len(direct))
    entries = dict(zip(grams, middle()))

    def entry(i, j):
        return entries[max(i, j), min(i, j)]

    state = Lanczos(w_a)
    x, r, p = [None] * (ITERS + 1), [one], [one]
    pad = [None]
    inverse = None

    def iterate(i):
        nonlocal x, r, p, inverse
        pivot = state.alphas[i] if i == 0 else state.alphas[i] - state.betas[i] * inverse
        inverse = 1.0 / pivot
        image = applied(p + pad, w_a + pad, w_b + pad, i + 2)
        gain = SCALE * inverse
        x = [added(q, times(gain, s)) for q, s in zip(x, p + pad * (ITERS + 1 - len(p)))]
        r = [minus(q, times(inverse, s)) for q, s in zip(r + pad, image)]
        if i + 1 < ITERS:
            ratio = state.betas[i + 1] * inverse * inverse
            p = [added(q, times(ratio, s)) for q, s in zip(r, p + pad)]

    for i in range(full + 1):
        state.row(i, [entries[i, j] for j in range(i + 1)])
        if i:
            iterate(i - 1)
    entries.update(zip(direct, late()))
    for i in range(full + 1, ITERS + 1):
        m = i - 1
        for j in range(i - 1):
            value = entry(m, j + 1) + (w_a[j] - w_a[m]) * entry(m, j) - w_b[m] * entry(m - 1, j)
            entries[i, j] = value + w_b[j] * entry(m, j - 1) if j else value
        state.row(i, [entries[i, j] for j in range(min(i + 1, ITERS))], i == ITERS)
        iterate(m)

    def store(ref):
        def put(i, j, value):
            band, within = i // SUB, lax.rem(i, SUB)
            ref[pl.ds(band * (tiles * SUB) + j * SUB + within, SUB, stride=J * SUB), :] = value

        return put

    combine(
        [
            (store(x_out), {w_slot(i): x[i] for i in range(ITERS)}),
            (store(r_out), {w_slot(i): r[i] for i in range(ITERS + 1)}),
        ],
        D, R,
    )
    for c, sends in pending:
        pl.when(sends)(c.wait_send)


def solution(mesh):
    nr, nc = mesh.shape["rows"], mesh.shape["cols"]

    def on_device(*inputs):
        rows, cols = inputs[0].shape
        bands, tiles, chunk = rows // SUB, cols // LANES, cols // (SUB * LANES)

        def pieces(a):
            return a.reshape(bands, SUB, tiles, LANES).transpose(0, 2, 1, 3).reshape(bands * tiles * SUB, LANES)

        def whole(a):
            return a.reshape(bands, tiles, SUB, LANES).transpose(0, 2, 1, 3).reshape(rows, cols)

        def held(*shape):
            return pltpu.VMEM(shape, jnp.float32)

        block = jax.ShapeDtypeStruct((bands * tiles * SUB, LANES), jnp.float32)
        high, tall = rows + 2 * DEPTH, rows + 2 * GHOST
        slots = SWITCH + ITERS + 1
        dma = pltpu.SemaphoreType.DMA
        x, r = pl.pallas_call(
            functools.partial(kernel, nr, nc, rows, cols),
            out_shape=(block, block),
            in_specs=[pl.BlockSpec(memory_space=pltpu.VMEM)] * 5,
            out_specs=[pl.BlockSpec(memory_space=pltpu.VMEM)] * 2,
            scratch_shapes=[
                held(slots, high, chunk, SUB, LANES),
                held(3, high, chunk, SUB, LANES),
                held(slots, 2, tall, LANES),
                held(3, 2, tall, LANES),
                held(DEPTH, tall, LANES),
                held(DEPTH, tall, LANES),
                held(2, bands, 4, SUB, LANES),
                held(bands, 4, SUB, LANES),
                held(bands, 4, SUB, LANES),
                held(96, LANES),
                held(3, nr * nc, 1, LANES),
                dma((COPIES,)), dma((COPIES,)), dma((3, nr * nc)), dma((3, nr * nc)),
            ],
            compiler_params=pltpu.CompilerParams(collective_id=0, has_side_effects=True),
        )(*(pieces(a) for a in inputs))
        return whole(x), whole(r)

    spec = P("rows", "cols")
    return jax.shard_map(
        on_device, mesh=mesh, in_specs=(spec,) * 5, out_specs=(spec, spec), check_vma=False
    )
```

```python
import functools

import jax
import jax.numpy as jnp
from jax import lax
from jax.experimental import pallas as pl
from jax.experimental.pallas import tpu as pltpu
from jax.sharding import PartitionSpec as P

ITERS = 12

prior_weight = 0.1
smooth_weight = 2.0
LANES = 128
SUB = 8
HALF = LANES // 2
MESH = pl.DeviceIdType.MESH

SCALE = 0.25
CENTER = 9.0 * SCALE
SPREAD = 16.0 * SCALE * SCALE
BLOCKS = (2, 2, 3, 3, 2)
KNOWN = 4
SWITCH = 7
DEPTH = max(BLOCKS)
GHOST = SUB
COPIES = 64
MEETINGS = 16


def each(start, stop, body):
    if stop - start < 32:
        for k in range(start, stop):
            body(k)
    else:
        lax.fori_loop(start, stop, lambda k, c: (body(k), c)[1], 0)


class Lanczos:
    def __init__(self, a):
        self.a, self.lower, self.pivots, self.inverses = a, {}, [], []
        self.alphas, self.betas = [], [None]

    def row(self, k, entries, last=False):
        reduced = []
        for j in range(k):
            value = entries[j]
            for i in range(j):
                value = value - reduced[i] * self.lower[j, i]
            reduced.append(value)
            self.lower[k, j] = value * self.inverses[j]
        if k:
            value = self.a[k - 1] + self.lower[k, k - 1]
            self.alphas.append(value - self.lower[k - 1, k - 2] if k > 1 else value)
        if last:
            return
        pivot = entries[k]
        for i in range(k):
            pivot = pivot - reduced[i] * self.lower[k, i]
        if k:
            self.betas.append(pivot * self.inverses[-1])
        self.pivots.append(pivot)
        self.inverses.append(1.0 / pivot)


def added(x, y):
    return y if x is None else (x if y is None else x + y)


def times(c, x):
    return None if x is None or c is None else (x if isinstance(c, float) and c == 1.0 else c * x)


def minus(x, y):
    return x if y is None else (-y if x is None else x - y)


def applied(p, a, b, size):
    out = [None] * size
    for k, value in enumerate(p):
        if value is None:
            continue
        out[k] = added(out[k], times(a[k], value))
        if k + 1 < size:
            out[k + 1] = added(out[k + 1], value)
        if k:
            out[k - 1] = added(out[k - 1], times(b[k], value))
    return out


def kernel(
    nr, nc, rows, cols,
    depth_in, mask_in, count_in, grad_h_in, grad_v_in,
    x_out, r_out,
    depth, hit_mask, hit_count, grad_h, grad_v,
    basis, coef, strip, strip_coef, strip_next, strip_flow,
    edge_send, edge_left, edge_right, folds, by_device,
    load, greet, send, recv, sum_send, sum_recv,
):
    me_r = lax.axis_index("rows")
    me_c = lax.axis_index("cols")
    J = cols // (SUB * LANES)
    tiles = cols // LANES
    R, D = rows, DEPTH
    bands = rows // SUB
    tall = rows + 2 * GHOST
    has_above, has_below = me_r > 0, me_r < nr - 1
    has_left, has_right = me_c > 0, me_c < nc - 1
    up, down = (me_r - 1, me_c), (me_r + 1, me_c)
    lefthand, righthand = (me_r, me_c - 1), (me_r, me_c + 1)
    devices = nr * nc
    me = me_r * nc + me_c

    def peer(k):
        other = lax.rem(me + k, devices)
        return (other // nc, lax.rem(other, nc))

    def meet(semaphore, along_rows, along_cols):
        ways = []
        for far, others, me_there, there in (
            (along_rows, nr, me_r, lambda k: (me_r + k, me_c)), (along_cols, nc, me_c, lambda k: (me_r, me_c + k)),
        ):
            if 0 < far < others:
                ways += [(me_there >= far, there(-far)), (me_there < others - far, there(far))]
        for exists, to in ways:
            @pl.when(exists)
            def _():
                pl.semaphore_signal(semaphore, inc=1, device_id=to, device_id_type=MESH)
        count = sum(exists.astype(jnp.int32) for exists, _ in ways)
        return lambda: pl.semaphore_wait(semaphore, count)

    barrier = pltpu.get_barrier_semaphore()
    greeted = meet(barrier, 1, 1)
    loads = [
        pltpu.make_async_copy(a, b, load.at[n])
        for n, (a, b) in enumerate(
            ((grad_h_in, grad_h), (grad_v_in, grad_v), (mask_in, hit_mask), (count_in, hit_count), (depth_in, depth))
        )
    ]
    for c in loads:
        c.start()

    meetings = []
    for axis, others in ((0, nr), (1, nc)):
        far = 1
        while far < others - 1 or (axis and far == 1 and others > 1):
            meetings.append((far, 0) if axis == 0 else (0, far))
            far *= 2
    met = [0, None]

    def meet_on():
        if met[1] is not None:
            met[1]()
            met[1] = None
        if met[0] < len(meetings):
            met[1] = meet(greet.at[met[0]], *meetings[met[0]])
            met[0] += 1

    sub_id = lax.broadcasted_iota(jnp.int32, (SUB, LANES), 0)
    lane_id = lax.broadcasted_iota(jnp.int32, (SUB, LANES), 1)
    zero = jnp.zeros((SUB, LANES), jnp.float32)

    used = [0]
    pending = []

    def copy(src, dst, to, sends, receives):
        k = used[0]
        used[0] += 1
        c = pltpu.make_async_remote_copy(
            src_ref=src, dst_ref=dst, send_sem=send.at[k], recv_sem=recv.at[k], device_id=to, device_id_type=MESH
        )
        pl.when(sends)(c.start)
        pending.append((c, sends))
        return c, receives

    def arrive(copies):
        for c, receives in copies:
            pl.when(receives)(c.wait_recv)

    def local(read, last_col, last_row):
        confidence = (read(hit_mask) * read(hit_count)).astype(jnp.float32) + prior_weight
        h, v = read(grad_h), read(grad_v)
        e = (SCALE * smooth_weight) * jnp.exp(-0.5 * h * h)
        s = (SCALE * smooth_weight) * jnp.exp(-0.5 * v * v)
        if last_col is not None:
            e = jnp.where(jnp.logical_and(last_col, jnp.logical_not(has_right)), 0.0, e)
        if last_row is not None:
            s = jnp.where(jnp.logical_and(last_row, jnp.logical_not(has_below)), 0.0, s)
        return SCALE * confidence, e, s, confidence * read(depth)

    for c in loads:
        c.wait()
    for side in range(2):
        tile = (tiles - 1) * side
        for band in range(bands):
            start = (band * tiles + tile) * SUB
            values = local(
                lambda ref: ref[start : start + SUB, :],
                lane_id == LANES - 1 if side else None,
                sub_id == SUB - 1 if band == bands - 1 else None,
            )
            for n, value in enumerate(values):
                edge_send[side, band, n] = value

    def row_coefficients(r, last_row):
        band, within = r // SUB, lax.rem(r, SUB)
        for j in range(J):
            start = band * (tiles * SUB) + j * SUB + within
            c, e, s, b = local(
                lambda ref: ref[pl.ds(start, SUB, stride=J * SUB), :],
                jnp.logical_and(lane_id == LANES - 1, sub_id == SUB - 1) if j == J - 1 else None,
                sub_id >= 0 if last_row else None,
            )
            coef[0, D + r, j] = c
            coef[1, D + r, j] = e
            coef[2, D + r, j] = s
            basis[0, D + r, j] = b

    def coefficient_rows(start, stop, last=False):
        for r in range(start, stop):
            row_coefficients(r, last and r == R - 1)

    def inner_coefficients():
        pairs = (R - 2 * D) // 2
        lax.fori_loop(0, pairs, lambda i, c: ([row_coefficients(D + 2 * i + t, False) for t in range(2)], c)[1], 0)
        coefficient_rows(D + 2 * pairs, R - D)

    coefficient_rows(0, D)
    coefficient_rows(R - D, R, True)

    def clear_ghost(first, strip_first):
        def _():
            for t in range(D):
                for j in range(J):
                    for n in range(3):
                        coef[n, first + t, j] = zero
                    for slot in exchanged:
                        basis[slot, first + t, j] = zero
            for side in range(2):
                for n in range(3):
                    strip_coef[n, side, strip_first : strip_first + GHOST, :] = zero
                for slot in strips_exchanged:
                    strip[slot, side, strip_first : strip_first + GHOST, :] = zero

        return _

    starts = [sum(BLOCKS[:n]) for n in range(len(BLOCKS))]

    def w_slot(k):
        return SWITCH + k if k else 0

    exchanged = sorted(
        {k if k < SWITCH else w_slot(k) for k in starts}
        | {(k - 1 if k < SWITCH else w_slot(k - 1)) for k in starts if k > 0}
        | set(range(SWITCH))
    )
    strips_exchanged = [0, w_slot(SWITCH - 1), w_slot(SWITCH)]
    pl.when(jnp.logical_not(has_above))(clear_ghost(0, 0))
    pl.when(jnp.logical_not(has_below))(clear_ghost(D + R, GHOST + R))

    @pl.when(jnp.logical_not(has_left))
    def _():
        edge_left[...] = jnp.zeros_like(edge_left)

    @pl.when(jnp.logical_not(has_right))
    def _():
        edge_right[...] = jnp.zeros_like(edge_right)

    greeted()

    def send_rows(slot, first, count):
        if count <= 0:
            return []
        top = D + first - 1
        bottom = D + R - (first - 1) - count
        return [
            copy(basis.at[slot, pl.ds(top, count)], basis.at[slot, pl.ds(top + R, count)], up, has_above, has_below),
            copy(basis.at[slot, pl.ds(bottom, count)], basis.at[slot, pl.ds(bottom - R, count)], down, has_below, has_above),
        ]

    def send_coefs(old, new):
        copies = []
        count = new - old
        bottom = D + R - new
        copies.append(copy(coef.at[2, pl.ds(bottom, count)], coef.at[2, pl.ds(bottom - R, count)], down, has_below, has_above))
        low, high = max(old, 1), new - 1
        if high >= low:
            n = high - low + 1
            top = D + low - 1
            bottom = D + R - high
            copies.append(copy(coef.at[:, pl.ds(top, n)], coef.at[:, pl.ds(top + R, n)], up, has_above, has_below))
            copies.append(
                copy(coef.at[0:2, pl.ds(bottom, n)], coef.at[0:2, pl.ds(bottom - R, n)], down, has_below, has_above)
            )
        return copies

    def send_strips(slots):
        copies = []
        for slot in slots:
            copies.append(
                copy(
                    strip.at[slot, :, pl.ds(GHOST, GHOST)], strip.at[slot, :, pl.ds(GHOST + R, GHOST)],
                    up, has_above, has_below,
                )
            )
            copies.append(
                copy(strip.at[slot, :, pl.ds(R, GHOST)], strip.at[slot, :, pl.ds(0, GHOST)], down, has_below, has_above)
            )
        return copies

    def rolled(v, shift, axis):
        return pltpu.roll(v, shift % v.shape[axis], axis)

    everywhere, inside = slice(0, tall), slice(GHOST, GHOST + R)

    def strip_ready(src, t, lines):
        v = strip[src, 0, lines, :]
        strip_flow[t, lines, :] = rolled(strip_coef[1, 0, lines, :] * (v - rolled(v, -1, 1)), 1, 1)
        strip_next[t, lines, :] = rolled(strip[src, 1, lines, :], -1, 1)

    def strip_step(src, prev, dst, a, b, lines):
        def spread(c):
            return c if isinstance(c, float) else jnp.concatenate([c] * ((lines.stop - lines.start) // SUB), axis=0)

        for side in range(2):
            v = strip[src, side, lines, :]
            flow = strip_coef[1, side, lines, :] * (v - rolled(v, -1, 1))
            fall = strip_coef[2, side, lines, :] * (v - rolled(v, -1, 0))
            value = (strip_coef[0, side, lines, :] - spread(a)) * v
            value = value + (flow - rolled(flow, 1, 1)) + (fall - rolled(fall, 1, 0))
            if b is not None:
                value = value - times(spread(b), strip[prev, side, lines, :])
            strip[dst, side, lines, :] = value

    def step(src, prev, dst, a, b, t, first, count, loop):
        def row(i, state):
            v, fall_above = state
            below = [basis[src, i + 1, j] for j in range(J)]
            fall = [coef[2, i, j] * (v[j] - below[j]) for j in range(J)]
            line = pl.ds(i + (GHOST - D), 1)
            to_left = [rolled(v[j], -1, 1) for j in range(J)]
            beyond = jnp.where(
                sub_id == SUB - 1, jnp.broadcast_to(strip_next[t, line, :], (SUB, LANES)), rolled(to_left[0], -1, 0)
            )
            flow = [
                coef[1, i, j] * (v[j] - jnp.where(lane_id == LANES - 1, to_left[j + 1] if j + 1 < J else beyond, to_left[j]))
                for j in range(J)
            ]
            to_right = [rolled(f, 1, 1) for f in flow]
            before = jnp.where(
                sub_id == 0, jnp.broadcast_to(strip_flow[t, line, :], (SUB, LANES)), rolled(to_right[J - 1], 1, 0)
            )
            for j in range(J):
                arriving = jnp.where(lane_id == 0, to_right[j - 1] if j else before, to_right[j])
                value = (coef[0, i, j] - a) * v[j] + ((flow[j] - arriving) + (fall[j] - fall_above[j]))
                if b is not None:
                    value = value - times(b, basis[prev, i, j])
                basis[dst, i, j] = value
            return below, fall

        v = [basis[src, first, j] for j in range(J)]
        state = v, [coef[2, first - 1, j] * (basis[src, first - 1, j] - v[j]) for j in range(J)]
        if not loop:
            for i in range(first, first + count):
                state = row(i, state)
            return
        unroll = next(u for u in (7, 6, 5, 4, 3, 2, 1) if count % u == 0)

        def body(n, state):
            for m in range(unroll):
                state = row(first + n * unroll + m, state)
            return state

        lax.fori_loop(0, count // unroll, body, state)

    def inner(recurrence, more, again):
        lines = inside if again else everywhere
        for t, (src, prev, dst, a, b) in enumerate(recurrence):
            strip_ready(src, t, lines)
            step(src, prev, dst, a, b, t, D + t + 1, R - 2 - 2 * t, True)
            if more or t + 1 < len(recurrence):
                strip_step(src, prev, dst, a, b, lines)

    def outer(recurrence, more, again):
        depth = len(recurrence)
        for t, (src, prev, dst, a, b) in enumerate(recurrence):
            if again:
                strip_ready(src, t, everywhere)
            step(src, prev, dst, a, b, t, D - (depth - 1 - t), depth, False)
            step(src, prev, dst, a, b, t, D + R - 1 - t, depth, False)
            if again and (more or t + 1 < depth):
                strip_step(src, prev, dst, a, b, everywhere)

    def dots(pairs, base):
        for g in range(0, len(pairs), 8):
            group = pairs[g : g + 8]
            slots = sorted({s for pair in group for s in pair})

            def body(i, sums):
                for j in range(J):
                    held = {s: basis[s, D + i, j] for s in slots}
                    sums = tuple(total + held[p] * held[q] for total, (p, q) in zip(sums, group))
                return sums

            sums = lax.fori_loop(0, R, body, (zero,) * len(group), unroll=2)
            for n, total in enumerate(sums):
                k = base + g + n
                folds[k : k + 1, :] = jnp.sum(total, axis=0, keepdims=True)

    def combine(targets, first, count):
        slots = sorted({s for _, terms in targets for s in terms})

        def body(i, c):
            for j in range(J):
                held = {s: basis[s, first + i, j] for s in slots}
                for target, terms in targets:
                    total = None
                    for s, weight in terms.items():
                        total = added(total, times(weight, held[s]))
                    if callable(target):
                        target(i, j, total)
                    else:
                        basis[target, first + i, j] = total
            return c

        lax.fori_loop(0, count, body, 0)

    def reduce(slot, count):
        n = -(-count // SUB) * SUB
        part = jnp.broadcast_to(jnp.sum(folds[0:n, :], axis=1, keepdims=True), (n, LANES))
        mine = lax.broadcasted_iota(jnp.int32, (n, LANES), 0) == lax.broadcasted_iota(jnp.int32, (n, LANES), 1)
        by_device[slot, me] = jnp.sum(jnp.where(mine, part, 0.0), axis=0, keepdims=True)

        def outgoing(k):
            here = by_device.at[slot, me]
            return pltpu.make_async_remote_copy(
                src_ref=here, dst_ref=here, send_sem=sum_send.at[slot, k], recv_sem=sum_recv.at[slot, me],
                device_id=peer(k), device_id_type=MESH,
            )

        each(1, devices, lambda k: outgoing(k).start())

        def finish():
            def arrival(k):
                source = lax.rem(me + k, devices)
                here = by_device.at[slot, source]
                pltpu.make_async_remote_copy(
                    src_ref=here, dst_ref=here, send_sem=sum_send.at[slot, k], recv_sem=sum_recv.at[slot, source],
                    device_id=peer(k), device_id_type=MESH,
                ).wait_recv()

            each(1, devices, arrival)
            each(1, devices, lambda k: outgoing(k).wait_send())
            if devices <= 32:
                parts = [by_device[slot, k] for k in range(devices)]
                while len(parts) > 1:
                    parts = [a + b for a, b in zip(parts[::2], parts[1::2])] + parts[len(parts) // 2 * 2 :]
                total = parts[0]
            else:
                total = lax.fori_loop(1, devices, lambda k, t: t + by_device[slot, k], by_device[slot, 0])
            return [jnp.broadcast_to(total[:, k : k + 1], (SUB, LANES)) for k in range(count)]

        return finish

    v_a = [CENTER] * SWITCH
    v_b = [None, 2.0 * SPREAD] + [SPREAD] * (SWITCH - 1)

    opening = send_rows(0, 1, BLOCKS[0]) + send_coefs(0, BLOCKS[0])
    sides = [
        copy(edge_send.at[0], edge_right, lefthand, has_left, has_right),
        copy(edge_send.at[1], edge_left, righthand, has_right, has_left),
    ]
    meet_on()
    inner_coefficients()
    arrive(sides)
    meet_on()
    for band in range(bands):
        own = slice(GHOST + band * SUB, GHOST + (band + 1) * SUB)
        for n in range(4):
            here = strip_coef.at[n] if n < 3 else strip.at[0]
            here[0, own, :] = jnp.where(lane_id < HALF, edge_send[0, band, n], edge_left[band, n])
            here[1, own, :] = jnp.where(lane_id < HALF, edge_right[band, n], edge_send[1, band, n])
    ghosts = send_strips([0]) + [
        copy(strip_coef.at[:, :, pl.ds(GHOST, GHOST)], strip_coef.at[:, :, pl.ds(GHOST + R, GHOST)], up, has_above, has_below),
        copy(strip_coef.at[:, :, pl.ds(R, GHOST)], strip_coef.at[:, :, pl.ds(0, GHOST)], down, has_below, has_above),
    ]
    deeper = []
    k = 0
    w_a = w_b = None
    one = jnp.ones((SUB, LANES), jnp.float32)
    for n, block in enumerate(BLOCKS):
        slot = (lambda i: i) if k < SWITCH else w_slot
        more = k + block < ITERS
        if n == 0:
            copies = opening + ghosts
        else:
            copies = send_rows(slot(k), 1, block) + send_rows(slot(k - 1), 2, block - 2)
            if k == SWITCH:
                copies = copies + send_strips([slot(k - 1), slot(k)])
            if n == 1 and BLOCKS[0] < D:
                deeper = send_coefs(BLOCKS[0], D)
        v_or_w = (v_a, v_b) if k < SWITCH else (w_a, w_b)
        recurrence = [
            (slot(i), slot(i - 1) if i else None, slot(i + 1), v_or_w[0][i], v_or_w[1][i]) for i in range(k, k + block)
        ]
        if k == KNOWN:
            pairs = [(i, j) for i in range(KNOWN + 1) for j in range(i + 1)]
            dots(pairs, 0)
            while met[1] is not None:
                meet_on()
            early = reduce(0, len(pairs))
        if k == SWITCH:
            combine(final, D + D, R - 2 * D)
        again = n == 0 or k == SWITCH
        inner(recurrence, more, again)
        if k < KNOWN:
            meet_on()
        if k == SWITCH:
            combine([(w_slot(i), {s: weights[i][s] for s in range(i + 1)}) for i in range(1, SWITCH - 1)], D, R)
            grams = [(i, j) for i in range(SWITCH + 1) for j in range(i + 1)]
            dots([(w_slot(i), w_slot(j)) for i, j in grams], 0)
        elif k > SWITCH:
            added_pairs = [(i, j) for i in range(starts[n - 1] + 1, k + 1) for j in range(i + 1)]
            dots([(w_slot(i), w_slot(j)) for i, j in added_pairs], len(grams))
            grams = grams + added_pairs
        if not more:
            middle = reduce(1, len(grams))
        arrive(copies)
        if k < KNOWN:
            meet_on()
        if block > BLOCKS[0] and deeper:
            arrive(deeper)
            deeper = []
        outer(recurrence, more, again)
        k += block
        if k == SWITCH:
            entries = dict(zip(pairs, early()))
            known = Lanczos(v_a)
            for i in range(KNOWN + 1):
                known.row(i, [entries[i, j] for j in range(i + 1)])
            w_a = known.alphas + [known.alphas[-1]] * (ITERS - KNOWN)
            w_b = known.betas + [known.betas[-1]] * (ITERS - KNOWN)
            weights = [[one]]
            for i in range(SWITCH):
                value = applied(weights[i] + [None], v_a + [None], v_b + [None], i + 2)
                value = [minus(p, times(w_a[i], q)) for p, q in zip(value, weights[i] + [None])]
                if i:
                    value = [minus(p, times(w_b[i], q)) for p, q in zip(value, weights[i - 1] + [None] * 2)]
                weights.append(value)
            final = [(w_slot(i), {s: weights[i][s] for s in range(i + 1)}) for i in (SWITCH - 1, SWITCH)]
            combine(final[:1], D - 1, 1)
            combine(final[:1], D + R, 1)
            combine(final, D, D)
            combine(final, D + R - D, D)
            for target, terms in final:
                for side in range(2):
                    for band in range(bands):
                        own = slice(GHOST + band * SUB, GHOST + (band + 1) * SUB)
                        total = None
                        for s, weight in terms.items():
                            total = added(total, times(weight, strip[s, side, own, :]))
                        strip[target, side, own, :] = total

    full = starts[-1]
    direct = [(i, j) for i in range(full + 1, ITERS + 1) for j in (i - 1, i) if j < ITERS]
    dots([(w_slot(i), w_slot(j)) for i, j in direct], 0)
    late = reduce(2, len(direct))
    entries = dict(zip(grams, middle()))

    def entry(i, j):
        return entries[max(i, j), min(i, j)]

    state = Lanczos(w_a)
    x, r, p = [None] * (ITERS + 1), [one], [one]
    pad = [None]
    inverse = None

    def iterate(i):
        nonlocal x, r, p, inverse
        pivot = state.alphas[i] if i == 0 else state.alphas[i] - state.betas[i] * inverse
        inverse = 1.0 / pivot
        image = applied(p + pad, w_a + pad, w_b + pad, i + 2)
        gain = SCALE * inverse
        x = [added(q, times(gain, s)) for q, s in zip(x, p + pad * (ITERS + 1 - len(p)))]
        r = [minus(q, times(inverse, s)) for q, s in zip(r + pad, image)]
        if i + 1 < ITERS:
            ratio = state.betas[i + 1] * inverse * inverse
            p = [added(q, times(ratio, s)) for q, s in zip(r, p + pad)]

    for i in range(full + 1):
        state.row(i, [entries[i, j] for j in range(i + 1)])
        if i:
            iterate(i - 1)
    entries.update(zip(direct, late()))
    for i in range(full + 1, ITERS + 1):
        m = i - 1
        for j in range(i - 1):
            value = entry(m, j + 1) + (w_a[j] - w_a[m]) * entry(m, j) - w_b[m] * entry(m - 1, j)
            entries[i, j] = value + w_b[j] * entry(m, j - 1) if j else value
        state.row(i, [entries[i, j] for j in range(min(i + 1, ITERS))], i == ITERS)
        iterate(m)

    def store(ref):
        def put(i, j, value):
            band, within = i // SUB, lax.rem(i, SUB)
            ref[pl.ds(band * (tiles * SUB) + j * SUB + within, SUB, stride=J * SUB), :] = value

        return put

    combine(
        [
            (store(x_out), {w_slot(i): x[i] for i in range(ITERS)}),
            (store(r_out), {w_slot(i): r[i] for i in range(ITERS + 1)}),
        ],
        D, R,
    )
    for c, sends in pending:
        pl.when(sends)(c.wait_send)


def solution(mesh):
    nr, nc = mesh.shape["rows"], mesh.shape["cols"]

    def on_device(*inputs):
        rows, cols = inputs[0].shape
        bands, tiles, chunk = rows // SUB, cols // LANES, cols // (SUB * LANES)

        def pieces(a):
            return a.reshape(bands, SUB, tiles, LANES).transpose(0, 2, 1, 3).reshape(bands * tiles * SUB, LANES)

        def whole(a):
            return a.reshape(bands, tiles, SUB, LANES).transpose(0, 2, 1, 3).reshape(rows, cols)

        def held(*shape):
            return pltpu.VMEM(shape, jnp.float32)

        block = jax.ShapeDtypeStruct((bands * tiles * SUB, LANES), jnp.float32)
        high, tall = rows + 2 * DEPTH, rows + 2 * GHOST
        slots = SWITCH + ITERS + 1
        dma = pltpu.SemaphoreType.DMA
        x, r = pl.pallas_call(
            functools.partial(kernel, nr, nc, rows, cols),
            out_shape=(block, block),
            in_specs=[pl.BlockSpec(memory_space=pl.ANY)] * 5,
            out_specs=[pl.BlockSpec(memory_space=pltpu.VMEM)] * 2,
            scratch_shapes=[pltpu.VMEM(block.shape, a.dtype) for a in inputs]
            + [
                held(slots, high, chunk, SUB, LANES),
                held(3, high, chunk, SUB, LANES),
                held(slots, 2, tall, LANES),
                held(3, 2, tall, LANES),
                held(DEPTH, tall, LANES),
                held(DEPTH, tall, LANES),
                held(2, bands, 4, SUB, LANES),
                held(bands, 4, SUB, LANES),
                held(bands, 4, SUB, LANES),
                held(96, LANES),
                held(3, nr * nc, 1, LANES),
                dma((5,)), pltpu.SemaphoreType.REGULAR((MEETINGS,)),
                dma((COPIES,)), dma((COPIES,)), dma((3, nr * nc)), dma((3, nr * nc)),
            ],
            compiler_params=pltpu.CompilerParams(collective_id=0, has_side_effects=True),
        )(*(pieces(a) for a in inputs))
        return whole(x), whole(r)

    spec = P("rows", "cols")
    return jax.shard_map(
        on_device, mesh=mesh, in_specs=(spec,) * 5, out_specs=(spec, spec), check_vma=False
    )
```

```python
import functools

import jax
import jax.numpy as jnp
from jax import lax
from jax.experimental import pallas as pl
from jax.experimental.pallas import tpu as pltpu
from jax.sharding import PartitionSpec as P

ITERS = 12

prior_weight = 0.1
smooth_weight = 2.0
LANES = 128
SUB = 8
HALF = LANES // 2
MESH = pl.DeviceIdType.MESH

SCALE = 0.25
CENTER = 9.0 * SCALE
SPREAD = 16.0 * SCALE * SCALE
BLOCKS = (2, 2, 3, 3, 2)
KNOWN = 4
SWITCH = 7
DEPTH = max(BLOCKS)
GHOST = SUB
COPIES = 64
MEETINGS = 16


def each(start, stop, body):
    if stop - start < 32:
        for k in range(start, stop):
            body(k)
    else:
        lax.fori_loop(start, stop, lambda k, c: (body(k), c)[1], 0)


class Lanczos:
    def __init__(self, a):
        self.a, self.lower, self.pivots, self.inverses = a, {}, [], []
        self.alphas, self.betas = [], [None]

    def row(self, k, entries, last=False):
        reduced = []
        for j in range(k):
            value = entries[j]
            for i in range(j):
                value = value - reduced[i] * self.lower[j, i]
            reduced.append(value)
            self.lower[k, j] = value * self.inverses[j]
        if k:
            value = self.a[k - 1] + self.lower[k, k - 1]
            self.alphas.append(value - self.lower[k - 1, k - 2] if k > 1 else value)
        if last:
            return
        pivot = entries[k]
        for i in range(k):
            pivot = pivot - reduced[i] * self.lower[k, i]
        if k:
            self.betas.append(pivot * self.inverses[-1])
        self.pivots.append(pivot)
        self.inverses.append(1.0 / pivot)


def added(x, y):
    return y if x is None else (x if y is None else x + y)


def times(c, x):
    return None if x is None or c is None else (x if isinstance(c, float) and c == 1.0 else c * x)


def minus(x, y):
    return x if y is None else (-y if x is None else x - y)


def chained(full, stop):
    return [(i, j) for i in range(full + 1, stop + 1) for j in (i - 1, i)]


def fill(entries, i, a, b):
    m = i - 1

    def entry(p, q):
        return entries[max(p, q), min(p, q)]

    for j in range(m):
        value = entry(m, j + 1) - times(b[m], entry(m - 1, j))
        if not (isinstance(a[j], float) and a[j] == a[m]):
            value = value + (a[j] - a[m]) * entry(m, j)
        entries[i, j] = value + times(b[j], entry(m, j - 1)) if j else value


def applied(p, a, b, size):
    out = [None] * size
    for k, value in enumerate(p):
        if value is None:
            continue
        out[k] = added(out[k], times(a[k], value))
        if k + 1 < size:
            out[k + 1] = added(out[k + 1], value)
        if k:
            out[k - 1] = added(out[k - 1], times(b[k], value))
    return out


def kernel(
    nr, nc, rows, cols,
    depth_in, mask_in, count_in, grad_h_in, grad_v_in,
    x_out, r_out,
    depth, hit_mask, hit_count, grad_h, grad_v,
    basis, coef, strip, strip_coef, strip_next, strip_flow,
    edge_send, edge_left, edge_right, folds, by_device,
    load, greet, send, recv, sum_send, sum_recv,
):
    me_r = lax.axis_index("rows")
    me_c = lax.axis_index("cols")
    J = cols // (SUB * LANES)
    tiles = cols // LANES
    R, D = rows, DEPTH
    bands = rows // SUB
    tall = rows + 2 * GHOST
    has_above, has_below = me_r > 0, me_r < nr - 1
    has_left, has_right = me_c > 0, me_c < nc - 1
    up, down = (me_r - 1, me_c), (me_r + 1, me_c)
    lefthand, righthand = (me_r, me_c - 1), (me_r, me_c + 1)
    devices = nr * nc
    me = me_r * nc + me_c

    def peer(k):
        other = lax.rem(me + k, devices)
        return (other // nc, lax.rem(other, nc))

    def meet(semaphore, along_rows, along_cols):
        ways = []
        for far, others, me_there, there in (
            (along_rows, nr, me_r, lambda k: (me_r + k, me_c)), (along_cols, nc, me_c, lambda k: (me_r, me_c + k)),
        ):
            if 0 < far < others:
                ways += [(me_there >= far, there(-far)), (me_there < others - far, there(far))]
        for exists, to in ways:
            @pl.when(exists)
            def _():
                pl.semaphore_signal(semaphore, inc=1, device_id=to, device_id_type=MESH)
        count = sum(exists.astype(jnp.int32) for exists, _ in ways)
        return lambda: pl.semaphore_wait(semaphore, count)

    barrier = pltpu.get_barrier_semaphore()
    greeted = meet(barrier, 1, 1)
    loads = [
        pltpu.make_async_copy(a, b, load.at[n])
        for n, (a, b) in enumerate(
            ((grad_h_in, grad_h), (grad_v_in, grad_v), (mask_in, hit_mask), (count_in, hit_count), (depth_in, depth))
        )
    ]
    for c in loads:
        c.start()

    meetings = []
    for axis, others in ((0, nr), (1, nc)):
        far = 1
        while far < others - 1 or (axis and far == 1 and others > 1):
            meetings.append((far, 0) if axis == 0 else (0, far))
            far *= 2
    met = [0, None]

    def meet_on():
        if met[1] is not None:
            met[1]()
            met[1] = None
        if met[0] < len(meetings):
            met[1] = meet(greet.at[met[0]], *meetings[met[0]])
            met[0] += 1

    sub_id = lax.broadcasted_iota(jnp.int32, (SUB, LANES), 0)
    lane_id = lax.broadcasted_iota(jnp.int32, (SUB, LANES), 1)
    zero = jnp.zeros((SUB, LANES), jnp.float32)

    used = [0]
    pending, reductions = [], []

    def copy(src, dst, to, sends, receives):
        k = used[0]
        used[0] += 1
        c = pltpu.make_async_remote_copy(
            src_ref=src, dst_ref=dst, send_sem=send.at[k], recv_sem=recv.at[k], device_id=to, device_id_type=MESH
        )
        pl.when(sends)(c.start)
        pending.append((c, sends))
        return c, receives

    def arrive(copies):
        for c, receives in copies:
            pl.when(receives)(c.wait_recv)

    def local(read, last_col, last_row):
        confidence = (read(hit_mask) * read(hit_count)).astype(jnp.float32) + prior_weight
        h, v = read(grad_h), read(grad_v)
        e = (SCALE * smooth_weight) * jnp.exp(-0.5 * h * h)
        s = (SCALE * smooth_weight) * jnp.exp(-0.5 * v * v)
        if last_col is not None:
            e = jnp.where(jnp.logical_and(last_col, jnp.logical_not(has_right)), 0.0, e)
        if last_row is not None:
            s = jnp.where(jnp.logical_and(last_row, jnp.logical_not(has_below)), 0.0, s)
        return SCALE * confidence, e, s, confidence * read(depth)

    for c in loads:
        c.wait()
    for side in range(2):
        tile = (tiles - 1) * side
        for band in range(bands):
            start = (band * tiles + tile) * SUB
            values = local(
                lambda ref: ref[start : start + SUB, :],
                lane_id == LANES - 1 if side else None,
                sub_id == SUB - 1 if band == bands - 1 else None,
            )
            for n, value in enumerate(values):
                edge_send[side, band, n] = value

    def row_coefficients(r, last_row):
        band, within = r // SUB, lax.rem(r, SUB)
        for j in range(J):
            start = band * (tiles * SUB) + j * SUB + within
            c, e, s, b = local(
                lambda ref: ref[pl.ds(start, SUB, stride=J * SUB), :],
                jnp.logical_and(lane_id == LANES - 1, sub_id == SUB - 1) if j == J - 1 else None,
                sub_id >= 0 if last_row else None,
            )
            coef[0, D + r, j] = c
            coef[1, D + r, j] = e
            coef[2, D + r, j] = s
            basis[0, D + r, j] = b

    def coefficient_rows(start, stop, last=False):
        for r in range(start, stop):
            row_coefficients(r, last and r == R - 1)

    def inner_coefficients():
        pairs = (R - 2 * D) // 2
        lax.fori_loop(0, pairs, lambda i, c: ([row_coefficients(D + 2 * i + t, False) for t in range(2)], c)[1], 0)
        coefficient_rows(D + 2 * pairs, R - D)

    coefficient_rows(0, D)
    coefficient_rows(R - D, R, True)

    def clear_ghost(first, strip_first):
        def _():
            for t in range(D):
                for j in range(J):
                    for n in range(3):
                        coef[n, first + t, j] = zero
                    for slot in exchanged:
                        basis[slot, first + t, j] = zero
            for n in range(3):
                strip_coef[n, strip_first : strip_first + GHOST, :] = zero
            for slot in strips_exchanged:
                strip[slot, strip_first : strip_first + GHOST, :] = zero

        return _

    starts = [sum(BLOCKS[:n]) for n in range(len(BLOCKS))]

    def w_slot(k):
        return SWITCH + k if k else 0

    exchanged = sorted(
        {k if k < SWITCH else w_slot(k) for k in starts}
        | {(k - 1 if k < SWITCH else w_slot(k - 1)) for k in starts if k > 0}
        | set(range(SWITCH))
    )
    strips_exchanged = [0, w_slot(SWITCH - 1), w_slot(SWITCH)]
    pl.when(jnp.logical_not(has_above))(clear_ghost(0, 0))
    pl.when(jnp.logical_not(has_below))(clear_ghost(D + R, GHOST + R))

    @pl.when(jnp.logical_not(has_left))
    def _():
        edge_left[...] = jnp.zeros_like(edge_left)

    @pl.when(jnp.logical_not(has_right))
    def _():
        edge_right[...] = jnp.zeros_like(edge_right)

    greeted()

    def send_rows(slot, first, count):
        if count <= 0:
            return []
        top = D + first - 1
        bottom = D + R - (first - 1) - count
        return [
            copy(basis.at[slot, pl.ds(top, count)], basis.at[slot, pl.ds(top + R, count)], up, has_above, has_below),
            copy(basis.at[slot, pl.ds(bottom, count)], basis.at[slot, pl.ds(bottom - R, count)], down, has_below, has_above),
        ]

    def send_coefs(old, new):
        copies = []
        count = new - old
        bottom = D + R - new
        copies.append(copy(coef.at[2, pl.ds(bottom, count)], coef.at[2, pl.ds(bottom - R, count)], down, has_below, has_above))
        low, high = max(old, 1), new - 1
        if high >= low:
            n = high - low + 1
            top = D + low - 1
            bottom = D + R - high
            copies.append(copy(coef.at[:, pl.ds(top, n)], coef.at[:, pl.ds(top + R, n)], up, has_above, has_below))
            copies.append(
                copy(coef.at[0:2, pl.ds(bottom, n)], coef.at[0:2, pl.ds(bottom - R, n)], down, has_below, has_above)
            )
        return copies

    def send_strips(slots):
        copies = []
        for slot in slots:
            copies.append(
                copy(
                    strip.at[slot, pl.ds(GHOST, GHOST)], strip.at[slot, pl.ds(GHOST + R, GHOST)],
                    up, has_above, has_below,
                )
            )
            copies.append(
                copy(strip.at[slot, pl.ds(R, GHOST)], strip.at[slot, pl.ds(0, GHOST)], down, has_below, has_above)
            )
        return copies

    def rolled(v, shift, axis):
        return pltpu.roll(v, shift % v.shape[axis], axis)

    everywhere, inside = slice(0, tall), slice(GHOST, GHOST + R)

    def strip_ready(src, t, lines):
        v = strip[src, lines, :]
        strip_flow[t, lines, :] = rolled(strip_coef[1, lines, :] * (v - rolled(v, -1, 1)), 1, 1)
        strip_next[t, lines, :] = rolled(v, HALF - 1, 1)

    def strip_step(src, prev, dst, a, b, lines):
        def spread(c):
            return c if isinstance(c, float) else jnp.concatenate([c] * ((lines.stop - lines.start) // SUB), axis=0)

        v = strip[src, lines, :]
        flow = strip_coef[1, lines, :] * (v - rolled(v, -1, 1))
        fall = strip_coef[2, lines, :] * (v - rolled(v, -1, 0))
        value = (strip_coef[0, lines, :] - spread(a)) * v
        value = value + (flow - rolled(flow, 1, 1)) + (fall - rolled(fall, 1, 0))
        if b is not None:
            value = value - times(spread(b), strip[prev, lines, :])
        strip[dst, lines, :] = value

    def step(src, prev, dst, a, b, t, first, count, loop):
        def row(i, state):
            v, fall_above = state
            below = [basis[src, i + 1, j] for j in range(J)]
            fall = [coef[2, i, j] * (v[j] - below[j]) for j in range(J)]
            line = pl.ds(i + (GHOST - D), 1)
            to_left = [rolled(v[j], -1, 1) for j in range(J)]
            beyond = jnp.where(
                sub_id == SUB - 1, jnp.broadcast_to(strip_next[t, line, :], (SUB, LANES)), rolled(to_left[0], -1, 0)
            )
            flow = [
                coef[1, i, j] * (v[j] - jnp.where(lane_id == LANES - 1, to_left[j + 1] if j + 1 < J else beyond, to_left[j]))
                for j in range(J)
            ]
            to_right = [rolled(f, 1, 1) for f in flow]
            before = jnp.where(
                sub_id == 0, jnp.broadcast_to(strip_flow[t, line, :], (SUB, LANES)), rolled(to_right[J - 1], 1, 0)
            )
            for j in range(J):
                arriving = jnp.where(lane_id == 0, to_right[j - 1] if j else before, to_right[j])
                value = (coef[0, i, j] - a) * v[j] + ((flow[j] - arriving) + (fall[j] - fall_above[j]))
                if b is not None:
                    value = value - times(b, basis[prev, i, j])
                basis[dst, i, j] = value
            return below, fall

        v = [basis[src, first, j] for j in range(J)]
        state = v, [coef[2, first - 1, j] * (basis[src, first - 1, j] - v[j]) for j in range(J)]
        if not loop:
            for i in range(first, first + count):
                state = row(i, state)
            return
        unroll = next(u for u in (7, 6, 5, 4, 3, 2, 1) if count % u == 0)

        def body(n, state):
            for m in range(unroll):
                state = row(first + n * unroll + m, state)
            return state

        lax.fori_loop(0, count // unroll, body, state)

    def inner(recurrence, more, again):
        lines = inside if again else everywhere
        for t, (src, prev, dst, a, b) in enumerate(recurrence):
            strip_ready(src, t, lines)
            step(src, prev, dst, a, b, t, D + t + 1, R - 2 - 2 * t, True)
            if more or t + 1 < len(recurrence):
                strip_step(src, prev, dst, a, b, lines)

    def outer(recurrence, more, again):
        depth = len(recurrence)
        for t, (src, prev, dst, a, b) in enumerate(recurrence):
            if again:
                strip_ready(src, t, everywhere)
            step(src, prev, dst, a, b, t, D - (depth - 1 - t), depth, False)
            step(src, prev, dst, a, b, t, D + R - 1 - t, depth, False)
            if again and (more or t + 1 < depth):
                strip_step(src, prev, dst, a, b, everywhere)

    def dots(pairs, base):
        for g in range(0, len(pairs), 8):
            group = pairs[g : g + 8]
            slots = sorted({s for pair in group for s in pair})

            def body(i, sums):
                for j in range(J):
                    held = {s: basis[s, D + i, j] for s in slots}
                    sums = tuple(total + held[p] * held[q] for total, (p, q) in zip(sums, group))
                return sums

            sums = lax.fori_loop(0, R, body, (zero,) * len(group), unroll=2)
            for n, total in enumerate(sums):
                k = base + g + n
                folds[k : k + 1, :] = jnp.sum(total, axis=0, keepdims=True)

    def combine(targets, first, count):
        slots = sorted({s for _, terms in targets for s in terms})

        def body(i, c):
            for j in range(J):
                held = {s: basis[s, first + i, j] for s in slots}
                for target, terms in targets:
                    total = None
                    for s, weight in terms.items():
                        total = added(total, times(weight, held[s]))
                    if callable(target):
                        target(i, j, total)
                    else:
                        basis[target, first + i, j] = total
            return c

        lax.fori_loop(0, count, body, 0)

    def reduce(slot, count):
        n = -(-count // SUB) * SUB
        part = jnp.broadcast_to(jnp.sum(folds[0:n, :], axis=1, keepdims=True), (n, LANES))
        mine = lax.broadcasted_iota(jnp.int32, (n, LANES), 0) == lax.broadcasted_iota(jnp.int32, (n, LANES), 1)
        by_device[slot, me] = jnp.sum(jnp.where(mine, part, 0.0), axis=0, keepdims=True)

        def outgoing(k):
            here = by_device.at[slot, me]
            return pltpu.make_async_remote_copy(
                src_ref=here, dst_ref=here, send_sem=sum_send.at[slot, k], recv_sem=sum_recv.at[slot, me],
                device_id=peer(k), device_id_type=MESH,
            )

        each(1, devices, lambda k: outgoing(k).start())
        reductions.append(outgoing)

        def finish():
            def arrival(k):
                source = lax.rem(me + k, devices)
                here = by_device.at[slot, source]
                pltpu.make_async_remote_copy(
                    src_ref=here, dst_ref=here, send_sem=sum_send.at[slot, k], recv_sem=sum_recv.at[slot, source],
                    device_id=peer(k), device_id_type=MESH,
                ).wait_recv()

            each(1, devices, arrival)
            if devices <= 32:
                parts = [by_device[slot, k] for k in range(devices)]
                while len(parts) > 1:
                    parts = [a + b for a, b in zip(parts[::2], parts[1::2])] + parts[len(parts) // 2 * 2 :]
                total = parts[0]
            else:
                total = lax.fori_loop(1, devices, lambda k, t: t + by_device[slot, k], by_device[slot, 0])
            return [jnp.broadcast_to(total[:, k : k + 1], (SUB, LANES)) for k in range(count)]

        return finish

    v_a = [CENTER] * SWITCH
    v_b = [None, 2.0 * SPREAD] + [SPREAD] * (SWITCH - 1)

    opening = send_rows(0, 1, BLOCKS[0]) + send_coefs(0, BLOCKS[0])
    sides = [
        copy(edge_send.at[0], edge_right, lefthand, has_left, has_right),
        copy(edge_send.at[1], edge_left, righthand, has_right, has_left),
    ]
    meet_on()
    inner_coefficients()
    arrive(sides)
    meet_on()
    for band in range(bands):
        own = slice(GHOST + band * SUB, GHOST + (band + 1) * SUB)
        for n in range(4):
            left_border = jnp.where(lane_id < HALF, edge_send[0, band, n], edge_left[band, n])
            right_border = jnp.where(lane_id < HALF, edge_right[band, n], edge_send[1, band, n])
            here = strip_coef.at[n] if n < 3 else strip.at[0]
            at_left = jnp.logical_or(lane_id < HALF // 2, lane_id >= LANES - HALF // 2)
            here[own, :] = jnp.where(at_left, left_border, rolled(right_border, HALF, 1))
    ghosts = send_strips([0]) + [
        copy(strip_coef.at[:, pl.ds(GHOST, GHOST)], strip_coef.at[:, pl.ds(GHOST + R, GHOST)], up, has_above, has_below),
        copy(strip_coef.at[:, pl.ds(R, GHOST)], strip_coef.at[:, pl.ds(0, GHOST)], down, has_below, has_above),
    ]
    deeper = []
    k = 0
    w_a = w_b = None
    one = jnp.ones((SUB, LANES), jnp.float32)
    for n, block in enumerate(BLOCKS):
        slot = (lambda i: i) if k < SWITCH else w_slot
        more = k + block < ITERS
        if k == KNOWN:
            while met[1] is not None:
                meet_on()
            base = starts[n - 1]
            direct = chained(base, KNOWN)
            dots(direct, len(pairs))
            pairs = pairs + direct
            early = reduce(0, len(pairs))
        if n == 0:
            copies = opening + ghosts
        else:
            copies = send_rows(slot(k), 1, block) + send_rows(slot(k - 1), 2, block - 2)
            if k == SWITCH:
                copies = copies + send_strips([slot(k - 1), slot(k)])
            if n == 1 and BLOCKS[0] < D:
                deeper = send_coefs(BLOCKS[0], D)
        v_or_w = (v_a, v_b) if k < SWITCH else (w_a, w_b)
        recurrence = [
            (slot(i), slot(i - 1) if i else None, slot(i + 1), v_or_w[0][i], v_or_w[1][i]) for i in range(k, k + block)
        ]
        if k == SWITCH:
            combine(final, D + D, R - 2 * D)
        again = n == 0 or k == SWITCH
        inner(recurrence, more, again)
        if k < KNOWN:
            meet_on()
        if k == SWITCH:
            combine([(w_slot(i), {s: weights[i][s] for s in range(i + 1)}) for i in range(1, SWITCH - 1)], D, R)
            grams = [(i, j) for i in range(SWITCH + 1) for j in range(i + 1)]
            dots([(w_slot(i), w_slot(j)) for i, j in grams], 0)
        elif k > SWITCH:
            added_pairs = [(i, j) for i in range(starts[n - 1] + 1, k + 1) for j in range(i + 1)]
            dots([(w_slot(i), w_slot(j)) for i, j in added_pairs], len(grams))
            grams = grams + added_pairs
        if not more:
            middle = reduce(1, len(grams))
        if k + block == KNOWN:
            pairs = [(i, j) for i in range(k + 1) for j in range(i + 1)]
            dots(pairs, 0)
        arrive(copies)
        if k < KNOWN:
            meet_on()
        if block > BLOCKS[0] and deeper:
            arrive(deeper)
            deeper = []
        outer(recurrence, more, again)
        k += block
        if k == SWITCH:
            entries = dict(zip(pairs, early()))
            known = Lanczos(v_a)
            for i in range(base + 1, KNOWN + 1):
                fill(entries, i, v_a, v_b)
            for i in range(KNOWN + 1):
                known.row(i, [entries[i, j] for j in range(i + 1)])
            w_a = known.alphas + [known.alphas[-1]] * (ITERS - KNOWN)
            w_b = known.betas + [known.betas[-1]] * (ITERS - KNOWN)
            weights = [[one]]
            for i in range(SWITCH):
                value = applied(weights[i] + [None], v_a + [None], v_b + [None], i + 2)
                value = [minus(p, times(w_a[i], q)) for p, q in zip(value, weights[i] + [None])]
                if i:
                    value = [minus(p, times(w_b[i], q)) for p, q in zip(value, weights[i - 1] + [None] * 2)]
                weights.append(value)
            final = [(w_slot(i), {s: weights[i][s] for s in range(i + 1)}) for i in (SWITCH - 1, SWITCH)]
            combine(final[:1], D - 1, 1)
            combine(final[:1], D + R, 1)
            combine(final, D, D)
            combine(final, D + R - D, D)
            for target, terms in final:
                for band in range(bands):
                    own = slice(GHOST + band * SUB, GHOST + (band + 1) * SUB)
                    total = None
                    for s, weight in terms.items():
                        total = added(total, times(weight, strip[s, own, :]))
                    strip[target, own, :] = total

    full = starts[-1]
    direct = chained(full, ITERS)[:-1]
    dots([(w_slot(i), w_slot(j)) for i, j in direct], 0)
    late = reduce(2, len(direct))
    entries = dict(zip(grams, middle()))

    state = Lanczos(w_a)
    x, r, p = [None] * (ITERS + 1), [one], [one]
    pad = [None]
    inverse = None

    def iterate(i):
        nonlocal x, r, p, inverse
        pivot = state.alphas[i] if i == 0 else state.alphas[i] - state.betas[i] * inverse
        inverse = 1.0 / pivot
        image = applied(p + pad, w_a + pad, w_b + pad, i + 2)
        gain = SCALE * inverse
        x = [added(q, times(gain, s)) for q, s in zip(x, p + pad * (ITERS + 1 - len(p)))]
        r = [minus(q, times(inverse, s)) for q, s in zip(r + pad, image)]
        if i + 1 < ITERS:
            ratio = state.betas[i + 1] * inverse * inverse
            p = [added(q, times(ratio, s)) for q, s in zip(r, p + pad)]

    for i in range(full + 1):
        state.row(i, [entries[i, j] for j in range(i + 1)])
        if i:
            iterate(i - 1)
    entries.update(zip(direct, late()))
    for i in range(full + 1, ITERS + 1):
        fill(entries, i, w_a, w_b)
        state.row(i, [entries[i, j] for j in range(min(i + 1, ITERS))], i == ITERS)
        iterate(i - 1)

    def store(ref):
        def put(i, j, value):
            band, within = i // SUB, lax.rem(i, SUB)
            ref[pl.ds(band * (tiles * SUB) + j * SUB + within, SUB, stride=J * SUB), :] = value

        return put

    combine(
        [
            (store(x_out), {w_slot(i): x[i] for i in range(ITERS)}),
            (store(r_out), {w_slot(i): r[i] for i in range(ITERS + 1)}),
        ],
        D, R,
    )
    for c, sends in pending:
        pl.when(sends)(c.wait_send)
    for outgoing in reductions:
        each(1, devices, lambda k: outgoing(k).wait_send())


def solution(mesh):
    nr, nc = mesh.shape["rows"], mesh.shape["cols"]

    def on_device(*inputs):
        rows, cols = inputs[0].shape
        bands, tiles, chunk = rows // SUB, cols // LANES, cols // (SUB * LANES)

        def pieces(a):
            return a.reshape(bands, SUB, tiles, LANES).transpose(0, 2, 1, 3).reshape(bands * tiles * SUB, LANES)

        def whole(a):
            return a.reshape(bands, tiles, SUB, LANES).transpose(0, 2, 1, 3).reshape(rows, cols)

        def held(*shape):
            return pltpu.VMEM(shape, jnp.float32)

        block = jax.ShapeDtypeStruct((bands * tiles * SUB, LANES), jnp.float32)
        high, tall = rows + 2 * DEPTH, rows + 2 * GHOST
        slots = SWITCH + ITERS + 1
        dma = pltpu.SemaphoreType.DMA
        x, r = pl.pallas_call(
            functools.partial(kernel, nr, nc, rows, cols),
            out_shape=(pltpu.VMEM(block.shape, jnp.float32),) * 2,
            in_specs=[pl.BlockSpec(memory_space=pl.ANY)] * 5,
            out_specs=[pl.BlockSpec(memory_space=pltpu.VMEM)] * 2,
            scratch_shapes=[pltpu.VMEM(block.shape, a.dtype) for a in inputs]
            + [
                held(slots, high, chunk, SUB, LANES),
                held(3, high, chunk, SUB, LANES),
                held(slots, tall, LANES),
                held(3, tall, LANES),
                held(DEPTH, tall, LANES),
                held(DEPTH, tall, LANES),
                held(2, bands, 4, SUB, LANES),
                held(bands, 4, SUB, LANES),
                held(bands, 4, SUB, LANES),
                held(96, LANES),
                held(3, nr * nc, 1, LANES),
                dma((5,)), pltpu.SemaphoreType.REGULAR((MEETINGS,)),
                dma((COPIES,)), dma((COPIES,)), dma((3, nr * nc)), dma((3, nr * nc)),
            ],
            compiler_params=pltpu.CompilerParams(collective_id=0, has_side_effects=True),
        )(*(pieces(a) for a in inputs))
        return whole(x), whole(r)

    spec = P("rows", "cols")
    return jax.shard_map(
        on_device, mesh=mesh, in_specs=(spec,) * 5, out_specs=(spec, spec), check_vma=False
    )
```

```python
import functools

import jax
import jax.numpy as jnp
from jax import lax
from jax.experimental import pallas as pl
from jax.experimental.pallas import tpu as pltpu
from jax.sharding import PartitionSpec as P

ITERS = 12

prior_weight = 0.1
smooth_weight = 2.0
LANES = 128
SUB = 8
HALF = LANES // 2
MESH = pl.DeviceIdType.MESH

SCALE = 0.25
CENTER = 9.0 * SCALE
SPREAD = 16.0 * SCALE * SCALE
BLOCKS = (2, 2, 3, 3, 2)
KNOWN = 4
SWITCH = 7
DEPTH = max(BLOCKS)
GHOST = SUB
COPIES = 64
MEETINGS = 16


def each(start, stop, body):
    if stop - start < 32:
        for k in range(start, stop):
            body(k)
    else:
        lax.fori_loop(start, stop, lambda k, c: (body(k), c)[1], 0)


class Lanczos:
    def __init__(self, a):
        self.a, self.lower, self.pivots, self.inverses = a, {}, [], []
        self.alphas, self.betas = [], [None]

    def row(self, k, entries, last=False):
        reduced = []
        for j in range(k):
            value = entries[j]
            for i in range(j):
                value = value - reduced[i] * self.lower[j, i]
            reduced.append(value)
            self.lower[k, j] = value * self.inverses[j]
        if k:
            value = self.a[k - 1] + self.lower[k, k - 1]
            self.alphas.append(value - self.lower[k - 1, k - 2] if k > 1 else value)
        if last:
            return
        pivot = entries[k]
        for i in range(k):
            pivot = pivot - reduced[i] * self.lower[k, i]
        if k:
            self.betas.append(pivot * self.inverses[-1])
        self.pivots.append(pivot)
        self.inverses.append(1.0 / pivot)


def added(x, y):
    return y if x is None else (x if y is None else x + y)


def times(c, x):
    return None if x is None or c is None else (x if isinstance(c, float) and c == 1.0 else c * x)


def minus(x, y):
    return x if y is None else (-y if x is None else x - y)


def chained(full, stop):
    return [(i, j) for i in range(full + 1, stop + 1) for j in (i - 1, i)]


def fill(entries, i, a, b):
    m = i - 1

    def entry(p, q):
        return entries[max(p, q), min(p, q)]

    for j in range(m):
        value = minus(entry(m, j + 1), times(b[m], entry(m - 1, j)))
        if not (isinstance(a[j], float) and a[j] == a[m]):
            value = value + (a[j] - a[m]) * entry(m, j)
        entries[i, j] = added(value, times(b[j], entry(m, j - 1))) if j else value


def applied(p, a, b, size):
    out = [None] * size
    for k, value in enumerate(p):
        if value is None:
            continue
        out[k] = added(out[k], times(a[k], value))
        if k + 1 < size:
            out[k + 1] = added(out[k + 1], value)
        if k:
            out[k - 1] = added(out[k - 1], times(b[k], value))
    return out


def kernel(
    nr, nc, rows, cols,
    depth_in, mask_in, count_in, grad_h_in, grad_v_in,
    x_out, r_out,
    depth, hit_mask, hit_count, grad_h, grad_v,
    basis, coef, strip, strip_coef, strip_next, strip_flow,
    edge_send, edge_left, edge_right, folds, by_device,
    load, greet, send, recv, sum_send, sum_recv,
):
    me_r = lax.axis_index("rows")
    me_c = lax.axis_index("cols")
    J = cols // (SUB * LANES)
    tiles = cols // LANES
    R, D = rows, DEPTH
    bands = rows // SUB
    tall = rows + 2 * GHOST
    has_above, has_below = me_r > 0, me_r < nr - 1
    has_left, has_right = me_c > 0, me_c < nc - 1
    up, down = (me_r - 1, me_c), (me_r + 1, me_c)
    lefthand, righthand = (me_r, me_c - 1), (me_r, me_c + 1)
    devices = nr * nc
    me = me_r * nc + me_c

    def peer(k):
        other = lax.rem(me + k, devices)
        return (other // nc, lax.rem(other, nc))

    def meet(semaphore, along_rows, along_cols):
        ways = []
        for far, others, me_there, there in (
            (along_rows, nr, me_r, lambda k: (me_r + k, me_c)), (along_cols, nc, me_c, lambda k: (me_r, me_c + k)),
        ):
            if 0 < far < others:
                ways += [(me_there >= far, there(-far)), (me_there < others - far, there(far))]
        for exists, to in ways:
            @pl.when(exists)
            def _():
                pl.semaphore_signal(semaphore, inc=1, device_id=to, device_id_type=MESH)
        count = sum(exists.astype(jnp.int32) for exists, _ in ways)
        return lambda: pl.semaphore_wait(semaphore, count)

    barrier = pltpu.get_barrier_semaphore()
    greeted = meet(barrier, 1, 1)
    loads = [
        pltpu.make_async_copy(a, b, load.at[n])
        for n, (a, b) in enumerate(
            ((grad_h_in, grad_h), (grad_v_in, grad_v), (mask_in, hit_mask), (count_in, hit_count), (depth_in, depth))
        )
    ]
    for c in loads:
        c.start()

    meetings = []
    for axis, others in ((0, nr), (1, nc)):
        far = 1
        while far < others - 1 or (axis and far == 1 and others > 1):
            meetings.append((far, 0) if axis == 0 else (0, far))
            far *= 2
    met = [0, None]

    def meet_on():
        if met[1] is not None:
            met[1]()
            met[1] = None
        if met[0] < len(meetings):
            met[1] = meet(greet.at[met[0]], *meetings[met[0]])
            met[0] += 1

    sub_id = lax.broadcasted_iota(jnp.int32, (SUB, LANES), 0)
    lane_id = lax.broadcasted_iota(jnp.int32, (SUB, LANES), 1)
    zero = jnp.zeros((SUB, LANES), jnp.float32)

    used = [0]
    pending, reductions = [], []

    def copy(src, dst, to, sends, receives):
        k = used[0]
        used[0] += 1
        c = pltpu.make_async_remote_copy(
            src_ref=src, dst_ref=dst, send_sem=send.at[k], recv_sem=recv.at[k], device_id=to, device_id_type=MESH
        )
        pl.when(sends)(c.start)
        pending.append((c, sends))
        return c, receives

    def arrive(copies):
        for c, receives in copies:
            pl.when(receives)(c.wait_recv)

    def local(read, last_col, last_row):
        confidence = (read(hit_mask) * read(hit_count)).astype(jnp.float32) + prior_weight
        h, v = read(grad_h), read(grad_v)
        e = (SCALE * smooth_weight) * jnp.exp(-0.5 * h * h)
        s = (SCALE * smooth_weight) * jnp.exp(-0.5 * v * v)
        if last_col is not None:
            e = jnp.where(jnp.logical_and(last_col, jnp.logical_not(has_right)), 0.0, e)
        if last_row is not None:
            s = jnp.where(jnp.logical_and(last_row, jnp.logical_not(has_below)), 0.0, s)
        return SCALE * confidence, e, s, confidence * read(depth)

    for c in loads:
        c.wait()
    for side in range(2):
        tile = (tiles - 1) * side
        for band in range(bands):
            start = (band * tiles + tile) * SUB
            values = local(
                lambda ref: ref[start : start + SUB, :],
                lane_id == LANES - 1 if side else None,
                sub_id == SUB - 1 if band == bands - 1 else None,
            )
            for n, value in enumerate(values):
                edge_send[side, band, n] = value

    def row_coefficients(r, last_row):
        band, within = r // SUB, lax.rem(r, SUB)
        for j in range(J):
            start = band * (tiles * SUB) + j * SUB + within
            c, e, s, b = local(
                lambda ref: ref[pl.ds(start, SUB, stride=J * SUB), :],
                jnp.logical_and(lane_id == LANES - 1, sub_id == SUB - 1) if j == J - 1 else None,
                sub_id >= 0 if last_row else None,
            )
            coef[0, D + r, j] = c
            coef[1, D + r, j] = e
            coef[2, D + r, j] = s
            basis[0, D + r, j] = b

    def coefficient_rows(start, stop, last=False):
        for r in range(start, stop):
            row_coefficients(r, last and r == R - 1)

    def inner_coefficients():
        pairs = (R - 2 * D) // 2
        lax.fori_loop(0, pairs, lambda i, c: ([row_coefficients(D + 2 * i + t, False) for t in range(2)], c)[1], 0)
        coefficient_rows(D + 2 * pairs, R - D)

    coefficient_rows(0, D)
    coefficient_rows(R - D, R, True)

    def clear_ghost(first, strip_first):
        def _():
            for t in range(D):
                for j in range(J):
                    for n in range(3):
                        coef[n, first + t, j] = zero
                    for slot in exchanged:
                        basis[slot, first + t, j] = zero
            for n in range(3):
                strip_coef[n, strip_first : strip_first + GHOST, :] = zero
            for slot in strips_exchanged:
                strip[slot, strip_first : strip_first + GHOST, :] = zero

        return _

    starts = [sum(BLOCKS[:n]) for n in range(len(BLOCKS))]

    def w_slot(k):
        return SWITCH + k if k else 0

    exchanged = sorted(
        {k if k < SWITCH else w_slot(k) for k in starts}
        | {(k - 1 if k < SWITCH else w_slot(k - 1)) for k in starts if k > 0}
        | set(range(SWITCH))
    )
    strips_exchanged = [0, w_slot(SWITCH)]
    pl.when(jnp.logical_not(has_above))(clear_ghost(0, 0))
    pl.when(jnp.logical_not(has_below))(clear_ghost(D + R, GHOST + R))

    @pl.when(jnp.logical_not(has_left))
    def _():
        edge_left[...] = jnp.zeros_like(edge_left)

    @pl.when(jnp.logical_not(has_right))
    def _():
        edge_right[...] = jnp.zeros_like(edge_right)

    greeted()

    def send_rows(slot, first, count):
        if count <= 0:
            return []
        top = D + first - 1
        bottom = D + R - (first - 1) - count
        return [
            copy(basis.at[slot, pl.ds(top, count)], basis.at[slot, pl.ds(top + R, count)], up, has_above, has_below),
            copy(basis.at[slot, pl.ds(bottom, count)], basis.at[slot, pl.ds(bottom - R, count)], down, has_below, has_above),
        ]

    def send_coefs(old, new):
        copies = []
        count = new - old
        bottom = D + R - new
        copies.append(copy(coef.at[2, pl.ds(bottom, count)], coef.at[2, pl.ds(bottom - R, count)], down, has_below, has_above))
        low, high = max(old, 1), new - 1
        if high >= low:
            n = high - low + 1
            top = D + low - 1
            bottom = D + R - high
            copies.append(copy(coef.at[:, pl.ds(top, n)], coef.at[:, pl.ds(top + R, n)], up, has_above, has_below))
            copies.append(
                copy(coef.at[0:2, pl.ds(bottom, n)], coef.at[0:2, pl.ds(bottom - R, n)], down, has_below, has_above)
            )
        return copies

    def send_strips(slots):
        copies = []
        for slot in slots:
            copies.append(
                copy(
                    strip.at[slot, pl.ds(GHOST, GHOST)], strip.at[slot, pl.ds(GHOST + R, GHOST)],
                    up, has_above, has_below,
                )
            )
            copies.append(
                copy(strip.at[slot, pl.ds(R, GHOST)], strip.at[slot, pl.ds(0, GHOST)], down, has_below, has_above)
            )
        return copies

    def rolled(v, shift, axis):
        return pltpu.roll(v, shift % v.shape[axis], axis)

    everywhere, inside = slice(0, tall), slice(GHOST, GHOST + R)

    def strip_ready(src, t, lines):
        v = strip[src, lines, :]
        strip_flow[t, lines, :] = rolled(strip_coef[1, lines, :] * (v - rolled(v, -1, 1)), 1, 1)
        strip_next[t, lines, :] = rolled(v, HALF - 1, 1)

    def strip_step(src, prev, dst, a, b, lines):
        def spread(c):
            return c if isinstance(c, float) else jnp.concatenate([c] * ((lines.stop - lines.start) // SUB), axis=0)

        v = strip[src, lines, :]
        flow = strip_coef[1, lines, :] * (v - rolled(v, -1, 1))
        fall = strip_coef[2, lines, :] * (v - rolled(v, -1, 0))
        value = (strip_coef[0, lines, :] - spread(a)) * v
        value = value + (flow - rolled(flow, 1, 1)) + (fall - rolled(fall, 1, 0))
        if b is not None:
            value = value - times(spread(b), strip[prev, lines, :])
        strip[dst, lines, :] = value

    def step(src, prev, dst, a, b, t, first, count, loop):
        def row(i, state):
            v, fall_above = state
            below = [basis[src, i + 1, j] for j in range(J)]
            fall = [coef[2, i, j] * (v[j] - below[j]) for j in range(J)]
            line = pl.ds(i + (GHOST - D), 1)
            to_left = [rolled(v[j], -1, 1) for j in range(J)]
            beyond = jnp.where(
                sub_id == SUB - 1, jnp.broadcast_to(strip_next[t, line, :], (SUB, LANES)), rolled(to_left[0], -1, 0)
            )
            flow = [
                coef[1, i, j] * (v[j] - jnp.where(lane_id == LANES - 1, to_left[j + 1] if j + 1 < J else beyond, to_left[j]))
                for j in range(J)
            ]
            to_right = [rolled(f, 1, 1) for f in flow]
            before = jnp.where(
                sub_id == 0, jnp.broadcast_to(strip_flow[t, line, :], (SUB, LANES)), rolled(to_right[J - 1], 1, 0)
            )
            for j in range(J):
                arriving = jnp.where(lane_id == 0, to_right[j - 1] if j else before, to_right[j])
                value = (coef[0, i, j] - a) * v[j] + ((flow[j] - arriving) + (fall[j] - fall_above[j]))
                if b is not None:
                    value = value - times(b, basis[prev, i, j])
                basis[dst, i, j] = value
            return below, fall

        v = [basis[src, first, j] for j in range(J)]
        state = v, [coef[2, first - 1, j] * (basis[src, first - 1, j] - v[j]) for j in range(J)]
        if not loop:
            for i in range(first, first + count):
                state = row(i, state)
            return
        unroll = next(u for u in (7, 6, 5, 4, 3, 2, 1) if count % u == 0)

        def body(n, state):
            for m in range(unroll):
                state = row(first + n * unroll + m, state)
            return state

        lax.fori_loop(0, count // unroll, body, state)

    def inner(recurrence, more, again):
        lines = inside if again else everywhere
        for t, (src, prev, dst, a, b) in enumerate(recurrence):
            strip_ready(src, t, lines)
            step(src, prev, dst, a, b, t, D + t + 1, R - 2 - 2 * t, True)
            if more or t + 1 < len(recurrence):
                strip_step(src, prev, dst, a, b, lines)

    def outer(recurrence, more, again):
        depth = len(recurrence)
        for t, (src, prev, dst, a, b) in enumerate(recurrence):
            if again:
                strip_ready(src, t, everywhere)
            step(src, prev, dst, a, b, t, D - (depth - 1 - t), depth, False)
            step(src, prev, dst, a, b, t, D + R - 1 - t, depth, False)
            if again and (more or t + 1 < depth):
                strip_step(src, prev, dst, a, b, everywhere)

    def dots(pairs, base):
        for g in range(0, len(pairs), 8):
            group = pairs[g : g + 8]
            slots = sorted({s for pair in group for s in pair})

            def body(i, sums):
                for j in range(J):
                    held = {s: basis[s, D + i, j] for s in slots}
                    sums = tuple(total + held[p] * held[q] for total, (p, q) in zip(sums, group))
                return sums

            sums = lax.fori_loop(0, R, body, (zero,) * len(group), unroll=2)
            for n, total in enumerate(sums):
                k = base + g + n
                folds[k : k + 1, :] = jnp.sum(total, axis=0, keepdims=True)

    def combine(targets, first, count):
        slots = sorted({s for _, terms in targets for s in terms})

        def body(i, c):
            for j in range(J):
                held = {s: basis[s, first + i, j] for s in slots}
                for target, terms in targets:
                    total = None
                    for s, weight in terms.items():
                        total = added(total, times(weight, held[s]))
                    if callable(target):
                        target(i, j, total)
                    else:
                        basis[target, first + i, j] = total
            return c

        lax.fori_loop(0, count, body, 0)

    def reduce(slot, count):
        n = -(-count // SUB) * SUB
        part = jnp.broadcast_to(jnp.sum(folds[0:n, :], axis=1, keepdims=True), (n, LANES))
        mine = lax.broadcasted_iota(jnp.int32, (n, LANES), 0) == lax.broadcasted_iota(jnp.int32, (n, LANES), 1)
        by_device[slot, me] = jnp.sum(jnp.where(mine, part, 0.0), axis=0, keepdims=True)

        def outgoing(k):
            here = by_device.at[slot, me]
            return pltpu.make_async_remote_copy(
                src_ref=here, dst_ref=here, send_sem=sum_send.at[slot, k], recv_sem=sum_recv.at[slot, me],
                device_id=peer(k), device_id_type=MESH,
            )

        each(1, devices, lambda k: outgoing(k).start())
        reductions.append(outgoing)

        def finish():
            def arrival(k):
                source = lax.rem(me + k, devices)
                here = by_device.at[slot, source]
                pltpu.make_async_remote_copy(
                    src_ref=here, dst_ref=here, send_sem=sum_send.at[slot, k], recv_sem=sum_recv.at[slot, source],
                    device_id=peer(k), device_id_type=MESH,
                ).wait_recv()

            each(1, devices, arrival)
            if devices <= 32:
                parts = [by_device[slot, k] for k in range(devices)]
                while len(parts) > 1:
                    parts = [a + b for a, b in zip(parts[::2], parts[1::2])] + parts[len(parts) // 2 * 2 :]
                total = parts[0]
            else:
                total = lax.fori_loop(1, devices, lambda k, t: t + by_device[slot, k], by_device[slot, 0])
            return [jnp.broadcast_to(total[:, k : k + 1], (SUB, LANES)) for k in range(count)]

        return finish

    v_a = [CENTER] * SWITCH
    v_b = [None, 2.0 * SPREAD] + [SPREAD] * (SWITCH - 1)
    v_b[KNOWN] = None

    opening = send_rows(0, 1, BLOCKS[0]) + send_coefs(0, BLOCKS[0])
    sides = [
        copy(edge_send.at[0], edge_right, lefthand, has_left, has_right),
        copy(edge_send.at[1], edge_left, righthand, has_right, has_left),
    ]
    meet_on()
    inner_coefficients()
    arrive(sides)
    meet_on()
    for band in range(bands):
        own = slice(GHOST + band * SUB, GHOST + (band + 1) * SUB)
        for n in range(4):
            left_border = jnp.where(lane_id < HALF, edge_send[0, band, n], edge_left[band, n])
            right_border = jnp.where(lane_id < HALF, edge_right[band, n], edge_send[1, band, n])
            here = strip_coef.at[n] if n < 3 else strip.at[0]
            at_left = jnp.logical_or(lane_id < HALF // 2, lane_id >= LANES - HALF // 2)
            here[own, :] = jnp.where(at_left, left_border, rolled(right_border, HALF, 1))
    ghosts = send_strips([0]) + [
        copy(strip_coef.at[:, pl.ds(GHOST, GHOST)], strip_coef.at[:, pl.ds(GHOST + R, GHOST)], up, has_above, has_below),
        copy(strip_coef.at[:, pl.ds(R, GHOST)], strip_coef.at[:, pl.ds(0, GHOST)], down, has_below, has_above),
    ]
    deeper = []
    k = 0
    w_a = w_b = None
    one = jnp.ones((SUB, LANES), jnp.float32)
    for n, block in enumerate(BLOCKS):
        slot = (lambda i: i) if k < SWITCH else w_slot
        more = k + block < ITERS
        if k == KNOWN:
            while met[1] is not None:
                meet_on()
            base = starts[n - 1]
            direct = chained(base, KNOWN)
            dots(direct, len(pairs))
            pairs = pairs + direct
            early = reduce(0, len(pairs))
        if n == 0:
            copies = opening + ghosts
        else:
            copies = send_rows(slot(k), 1, block)
            if k == SWITCH:
                copies = copies + send_strips([slot(k)])
            elif k != KNOWN:
                copies = copies + send_rows(slot(k - 1), 2, block - 2)
            if n == 1 and BLOCKS[0] < D:
                deeper = send_coefs(BLOCKS[0], D)
        v_or_w = (v_a, v_b) if k < SWITCH else (w_a, w_b)
        recurrence = [
            (slot(i), slot(i - 1) if i else None, slot(i + 1), v_or_w[0][i], v_or_w[1][i]) for i in range(k, k + block)
        ]
        if k == SWITCH:
            combine(final, D + D, R - 2 * D)
        again = n == 0 or k == SWITCH
        inner(recurrence, more, again)
        if k < KNOWN:
            meet_on()
        if k == SWITCH:
            combine([(w_slot(i), {s: weights[i][s] for s in range(i + 1)}) for i in range(1, SWITCH)], D, R)
            grams = [(i, j) for i in range(SWITCH + 1) for j in range(i + 1)]
            dots([(w_slot(i), w_slot(j)) for i, j in grams], 0)
        elif k > SWITCH:
            added_pairs = chained(starts[n - 1], k)
            dots([(w_slot(i), w_slot(j)) for i, j in added_pairs], len(grams))
            grams = grams + added_pairs
        if not more:
            middle = reduce(1, len(grams))
        if k + block == KNOWN:
            pairs = [(i, j) for i in range(k + 1) for j in range(i + 1)]
            dots(pairs, 0)
        arrive(copies)
        if k < KNOWN:
            meet_on()
        if block > BLOCKS[0] and deeper:
            arrive(deeper)
            deeper = []
        outer(recurrence, more, again)
        k += block
        if k == SWITCH:
            entries = dict(zip(pairs, early()))
            known = Lanczos(v_a)
            for i in range(base + 1, KNOWN + 1):
                fill(entries, i, v_a, v_b)
            for i in range(KNOWN + 1):
                known.row(i, [entries[i, j] for j in range(i + 1)])
            w_a = known.alphas + [known.alphas[-1]] * (ITERS - KNOWN)
            w_b = known.betas + [known.betas[-1]] * (ITERS - KNOWN)
            weights = [[one]]
            for i in range(SWITCH):
                value = applied(weights[i] + [None], v_a + [None], v_b + [None], i + 2)
                value = [minus(p, times(w_a[i], q)) for p, q in zip(value, weights[i] + [None])]
                if i:
                    value = [minus(p, times(w_b[i], q)) for p, q in zip(value, weights[i - 1] + [None] * 2)]
                weights.append(value)
            w_b[SWITCH] = None
            final = [(w_slot(SWITCH), dict(enumerate(weights[SWITCH])))]
            combine(final, D, D)
            combine(final, D + R - D, D)
            for target, terms in final:
                for band in range(bands):
                    own = slice(GHOST + band * SUB, GHOST + (band + 1) * SUB)
                    total = None
                    for s, weight in terms.items():
                        total = added(total, times(weight, strip[s, own, :]))
                    strip[target, own, :] = total

    full = starts[-1]
    direct = chained(full, ITERS)[:-1]
    dots([(w_slot(i), w_slot(j)) for i, j in direct], 0)
    late = reduce(2, len(direct))
    entries = dict(zip(grams, middle()))

    state = Lanczos(w_a)
    x, r, p = [None] * (ITERS + 1), [one], [one]
    pad = [None]
    inverse = None

    def iterate(i):
        nonlocal x, r, p, inverse
        pivot = state.alphas[i] if i == 0 else state.alphas[i] - state.betas[i] * inverse
        inverse = 1.0 / pivot
        image = applied(p + pad, w_a + pad, w_b + pad, i + 2)
        gain = SCALE * inverse
        x = [added(q, times(gain, s)) for q, s in zip(x, p + pad * (ITERS + 1 - len(p)))]
        r = [minus(q, times(inverse, s)) for q, s in zip(r + pad, image)]
        if i + 1 < ITERS:
            ratio = state.betas[i + 1] * inverse * inverse
            p = [added(q, times(ratio, s)) for q, s in zip(r, p + pad)]

    for i in range(full + 1):
        if i > SWITCH:
            fill(entries, i, w_a, w_b)
        state.row(i, [entries[i, j] for j in range(i + 1)])
        if i:
            iterate(i - 1)
    entries.update(zip(direct, late()))
    for i in range(full + 1, ITERS + 1):
        fill(entries, i, w_a, w_b)
        state.row(i, [entries[i, j] for j in range(min(i + 1, ITERS))], i == ITERS)
        iterate(i - 1)

    def store(ref):
        def put(i, j, value):
            band, within = i // SUB, lax.rem(i, SUB)
            ref[pl.ds(band * (tiles * SUB) + j * SUB + within, SUB, stride=J * SUB), :] = value

        return put

    combine(
        [
            (store(x_out), {w_slot(i): x[i] for i in range(ITERS)}),
            (store(r_out), {w_slot(i): r[i] for i in range(ITERS + 1)}),
        ],
        D, R,
    )
    for c, sends in pending:
        pl.when(sends)(c.wait_send)
    for outgoing in reductions:
        each(1, devices, lambda k: outgoing(k).wait_send())


def solution(mesh):
    nr, nc = mesh.shape["rows"], mesh.shape["cols"]

    def on_device(*inputs):
        rows, cols = inputs[0].shape
        bands, tiles, chunk = rows // SUB, cols // LANES, cols // (SUB * LANES)

        def pieces(a):
            return a.reshape(bands, SUB, tiles, LANES).transpose(0, 2, 1, 3).reshape(bands * tiles * SUB, LANES)

        def whole(a):
            return a.reshape(bands, tiles, SUB, LANES).transpose(0, 2, 1, 3).reshape(rows, cols)

        def held(*shape):
            return pltpu.VMEM(shape, jnp.float32)

        block = jax.ShapeDtypeStruct((bands * tiles * SUB, LANES), jnp.float32)
        high, tall = rows + 2 * DEPTH, rows + 2 * GHOST
        slots = SWITCH + ITERS + 1
        dma = pltpu.SemaphoreType.DMA
        x, r = pl.pallas_call(
            functools.partial(kernel, nr, nc, rows, cols),
            out_shape=(pltpu.VMEM(block.shape, jnp.float32),) * 2,
            in_specs=[pl.BlockSpec(memory_space=pl.ANY)] * 5,
            out_specs=[pl.BlockSpec(memory_space=pltpu.VMEM)] * 2,
            scratch_shapes=[pltpu.VMEM(block.shape, a.dtype) for a in inputs]
            + [
                held(slots, high, chunk, SUB, LANES),
                held(3, high, chunk, SUB, LANES),
                held(slots, tall, LANES),
                held(3, tall, LANES),
                held(DEPTH, tall, LANES),
                held(DEPTH, tall, LANES),
                held(2, bands, 4, SUB, LANES),
                held(bands, 4, SUB, LANES),
                held(bands, 4, SUB, LANES),
                held(96, LANES),
                held(3, nr * nc, 1, LANES),
                dma((5,)), pltpu.SemaphoreType.REGULAR((MEETINGS,)),
                dma((COPIES,)), dma((COPIES,)), dma((3, nr * nc)), dma((3, nr * nc)),
            ],
            compiler_params=pltpu.CompilerParams(collective_id=0, has_side_effects=True),
        )(*(pieces(a) for a in inputs))
        return whole(x), whole(r)

    spec = P("rows", "cols")
    return jax.shard_map(
        on_device, mesh=mesh, in_specs=(spec,) * 5, out_specs=(spec, spec), check_vma=False
    )
```

```python
import functools

import jax
import jax.numpy as jnp
from jax import lax
from jax.experimental import pallas as pl
from jax.experimental.pallas import tpu as pltpu
from jax.sharding import PartitionSpec as P

ITERS = 12

prior_weight = 0.1
smooth_weight = 2.0
LANES = 128
SUB = 8
HALF = LANES // 2
MESH = pl.DeviceIdType.MESH

SCALE = 0.25
CENTER = 9.0 * SCALE
SPREAD = 16.0 * SCALE * SCALE
BLOCKS = (2, 2, 3, 3, 2)
KNOWN = 4
SWITCH = 7
DEPTH = max(BLOCKS)
GHOST = SUB
COPIES = 64
MEETINGS = 16


def each(start, stop, body):
    if stop - start < 32:
        for k in range(start, stop):
            body(k)
    else:
        lax.fori_loop(start, stop, lambda k, c: (body(k), c)[1], 0)


class Lanczos:
    def __init__(self, a):
        self.a, self.lower, self.pivots, self.inverses = a, {}, [], []
        self.alphas, self.betas = [], [None]

    def row(self, k, entries, last=False):
        reduced = []
        for j in range(k):
            value = entries[j]
            for i in range(j):
                value = value - reduced[i] * self.lower[j, i]
            reduced.append(value)
            self.lower[k, j] = value * self.inverses[j]
        if k:
            value = self.a[k - 1] + self.lower[k, k - 1]
            self.alphas.append(value - self.lower[k - 1, k - 2] if k > 1 else value)
        if last:
            return
        pivot = entries[k]
        for i in range(k):
            pivot = pivot - reduced[i] * self.lower[k, i]
        if k:
            self.betas.append(pivot * self.inverses[-1])
        self.pivots.append(pivot)
        self.inverses.append(1.0 / pivot)


def added(x, y):
    return y if x is None else (x if y is None else x + y)


def times(c, x):
    return None if x is None or c is None else (x if isinstance(c, float) and c == 1.0 else c * x)


def minus(x, y):
    return x if y is None else (-y if x is None else x - y)


def chained(full, stop):
    return [(i, j) for i in range(full + 1, stop + 1) for j in (i - 1, i)]


def fill(entries, i, a, b):
    m = i - 1

    def entry(p, q):
        return entries[max(p, q), min(p, q)]

    for j in range(m):
        value = minus(entry(m, j + 1), times(b[m], entry(m - 1, j)))
        if not (isinstance(a[j], float) and a[j] == a[m]):
            value = value + (a[j] - a[m]) * entry(m, j)
        entries[i, j] = added(value, times(b[j], entry(m, j - 1))) if j else value


def applied(p, a, b, size):
    out = [None] * size
    for k, value in enumerate(p):
        if value is None:
            continue
        out[k] = added(out[k], times(a[k], value))
        if k + 1 < size:
            out[k + 1] = added(out[k + 1], value)
        if k:
            out[k - 1] = added(out[k - 1], times(b[k], value))
    return out


def kernel(
    nr, nc, rows, cols,
    depth_in, mask_in, count_in, grad_h_in, grad_v_in,
    both_out,
    depth, hit_mask, hit_count, grad_h, grad_v,
    basis, coef, strip, strip_coef, strip_next, strip_flow,
    edge_send, edge_left, edge_right, folds, by_device,
    load, greet, send, recv, sum_send, sum_recv,
):
    x_out, r_out = both_out.at[0], both_out.at[1]
    me_r = lax.axis_index("rows")
    me_c = lax.axis_index("cols")
    J = cols // (SUB * LANES)
    tiles = cols // LANES
    R, D = rows, DEPTH
    bands = rows // SUB
    tall = rows + 2 * GHOST
    has_above, has_below = me_r > 0, me_r < nr - 1
    has_left, has_right = me_c > 0, me_c < nc - 1
    up, down = (me_r - 1, me_c), (me_r + 1, me_c)
    lefthand, righthand = (me_r, me_c - 1), (me_r, me_c + 1)
    devices = nr * nc
    me = me_r * nc + me_c

    def peer(k):
        other = lax.rem(me + k, devices)
        return (other // nc, lax.rem(other, nc))

    def meet(semaphore, along_rows, along_cols):
        ways = []
        for far, others, me_there, there in (
            (along_rows, nr, me_r, lambda k: (me_r + k, me_c)), (along_cols, nc, me_c, lambda k: (me_r, me_c + k)),
        ):
            if 0 < far < others:
                ways += [(me_there >= far, there(-far)), (me_there < others - far, there(far))]
        for exists, to in ways:
            @pl.when(exists)
            def _():
                pl.semaphore_signal(semaphore, inc=1, device_id=to, device_id_type=MESH)
        count = sum(exists.astype(jnp.int32) for exists, _ in ways)
        return lambda: pl.semaphore_wait(semaphore, count)

    barrier = pltpu.get_barrier_semaphore()
    greeted = meet(barrier, 1, 1)
    loads = [
        pltpu.make_async_copy(a, b, load.at[n])
        for n, (a, b) in enumerate(
            ((grad_h_in, grad_h), (grad_v_in, grad_v), (mask_in, hit_mask), (count_in, hit_count), (depth_in, depth))
        )
    ]
    for c in loads:
        c.start()

    meetings = []
    for axis, others in ((0, nr), (1, nc)):
        far = 1
        while far < others - 1 or (axis and far == 1 and others > 1):
            meetings.append((far, 0) if axis == 0 else (0, far))
            far *= 2
    met = [0, None]

    def meet_on():
        if met[1] is not None:
            met[1]()
            met[1] = None
        if met[0] < len(meetings):
            met[1] = meet(greet.at[met[0]], *meetings[met[0]])
            met[0] += 1

    sub_id = lax.broadcasted_iota(jnp.int32, (SUB, LANES), 0)
    lane_id = lax.broadcasted_iota(jnp.int32, (SUB, LANES), 1)
    zero = jnp.zeros((SUB, LANES), jnp.float32)

    used = [0]
    pending, reductions = [], []

    def copy(src, dst, to, sends, receives):
        k = used[0]
        used[0] += 1
        c = pltpu.make_async_remote_copy(
            src_ref=src, dst_ref=dst, send_sem=send.at[k], recv_sem=recv.at[k], device_id=to, device_id_type=MESH
        )
        pl.when(sends)(c.start)
        pending.append((c, sends))
        return c, receives

    def arrive(copies):
        for c, receives in copies:
            pl.when(receives)(c.wait_recv)

    def local(read, last_col, last_row):
        confidence = (read(hit_mask) * read(hit_count)).astype(jnp.float32) + prior_weight
        h, v = read(grad_h), read(grad_v)
        e = (SCALE * smooth_weight) * jnp.exp(-0.5 * h * h)
        s = (SCALE * smooth_weight) * jnp.exp(-0.5 * v * v)
        if last_col is not None:
            e = jnp.where(jnp.logical_and(last_col, jnp.logical_not(has_right)), 0.0, e)
        if last_row is not None:
            s = jnp.where(jnp.logical_and(last_row, jnp.logical_not(has_below)), 0.0, s)
        return SCALE * confidence, e, s, confidence * read(depth)

    for c in loads:
        c.wait()
    for side in range(2):
        tile = (tiles - 1) * side
        for band in range(bands):
            start = (band * tiles + tile) * SUB
            values = local(
                lambda ref: ref[start : start + SUB, :],
                lane_id == LANES - 1 if side else None,
                sub_id == SUB - 1 if band == bands - 1 else None,
            )
            for n, value in enumerate(values):
                edge_send[side, band, n] = value

    def row_coefficients(r, last_row):
        band, within = r // SUB, lax.rem(r, SUB)
        for j in range(J):
            start = band * (tiles * SUB) + j * SUB + within
            c, e, s, b = local(
                lambda ref: ref[pl.ds(start, SUB, stride=J * SUB), :],
                jnp.logical_and(lane_id == LANES - 1, sub_id == SUB - 1) if j == J - 1 else None,
                sub_id >= 0 if last_row else None,
            )
            coef[0, D + r, j] = c
            coef[1, D + r, j] = e
            coef[2, D + r, j] = s
            basis[0, D + r, j] = b

    def coefficient_rows(start, stop, last=False):
        for r in range(start, stop):
            row_coefficients(r, last and r == R - 1)

    def inner_coefficients():
        pairs = (R - 2 * D) // 2
        lax.fori_loop(0, pairs, lambda i, c: ([row_coefficients(D + 2 * i + t, False) for t in range(2)], c)[1], 0)
        coefficient_rows(D + 2 * pairs, R - D)

    coefficient_rows(0, D)
    coefficient_rows(R - D, R, True)

    def clear_ghost(first, strip_first):
        def _():
            for t in range(D):
                for j in range(J):
                    for n in range(3):
                        coef[n, first + t, j] = zero
                    for slot in exchanged:
                        basis[slot, first + t, j] = zero
            for n in range(3):
                strip_coef[n, strip_first : strip_first + GHOST, :] = zero
            for slot in strips_exchanged:
                strip[slot, strip_first : strip_first + GHOST, :] = zero

        return _

    starts = [sum(BLOCKS[:n]) for n in range(len(BLOCKS))]

    def w_slot(k):
        return SWITCH + k if k else 0

    exchanged = sorted(
        {k if k < SWITCH else w_slot(k) for k in starts}
        | {(k - 1 if k < SWITCH else w_slot(k - 1)) for k in starts if k > 0}
        | set(range(SWITCH))
    )
    strips_exchanged = [0, w_slot(SWITCH)]
    pl.when(jnp.logical_not(has_above))(clear_ghost(0, 0))
    pl.when(jnp.logical_not(has_below))(clear_ghost(D + R, GHOST + R))

    @pl.when(jnp.logical_not(has_left))
    def _():
        edge_left[...] = jnp.zeros_like(edge_left)

    @pl.when(jnp.logical_not(has_right))
    def _():
        edge_right[...] = jnp.zeros_like(edge_right)

    greeted()

    def send_rows(slot, first, count):
        if count <= 0:
            return []
        top = D + first - 1
        bottom = D + R - (first - 1) - count
        return [
            copy(basis.at[slot, pl.ds(top, count)], basis.at[slot, pl.ds(top + R, count)], up, has_above, has_below),
            copy(basis.at[slot, pl.ds(bottom, count)], basis.at[slot, pl.ds(bottom - R, count)], down, has_below, has_above),
        ]

    def send_coefs(old, new):
        copies = []
        count = new - old
        bottom = D + R - new
        copies.append(copy(coef.at[2, pl.ds(bottom, count)], coef.at[2, pl.ds(bottom - R, count)], down, has_below, has_above))
        low, high = max(old, 1), new - 1
        if high >= low:
            n = high - low + 1
            top = D + low - 1
            bottom = D + R - high
            copies.append(copy(coef.at[:, pl.ds(top, n)], coef.at[:, pl.ds(top + R, n)], up, has_above, has_below))
            copies.append(
                copy(coef.at[0:2, pl.ds(bottom, n)], coef.at[0:2, pl.ds(bottom - R, n)], down, has_below, has_above)
            )
        return copies

    def send_strips(slots):
        copies = []
        for slot in slots:
            copies.append(
                copy(
                    strip.at[slot, pl.ds(GHOST, GHOST)], strip.at[slot, pl.ds(GHOST + R, GHOST)],
                    up, has_above, has_below,
                )
            )
            copies.append(
                copy(strip.at[slot, pl.ds(R, GHOST)], strip.at[slot, pl.ds(0, GHOST)], down, has_below, has_above)
            )
        return copies

    def rolled(v, shift, axis):
        return pltpu.roll(v, shift % v.shape[axis], axis)

    everywhere, inside = slice(0, tall), slice(GHOST, GHOST + R)

    def strip_ready(src, t, lines):
        v = strip[src, lines, :]
        strip_flow[t, lines, :] = rolled(strip_coef[1, lines, :] * (v - rolled(v, -1, 1)), 1, 1)
        strip_next[t, lines, :] = rolled(v, HALF - 1, 1)

    def strip_step(src, prev, dst, a, b, lines):
        def spread(c):
            return c if isinstance(c, float) else jnp.concatenate([c] * ((lines.stop - lines.start) // SUB), axis=0)

        v = strip[src, lines, :]
        flow = strip_coef[1, lines, :] * (v - rolled(v, -1, 1))
        fall = strip_coef[2, lines, :] * (v - rolled(v, -1, 0))
        value = (strip_coef[0, lines, :] - spread(a)) * v
        value = value + (flow - rolled(flow, 1, 1)) + (fall - rolled(fall, 1, 0))
        if b is not None:
            value = value - times(spread(b), strip[prev, lines, :])
        strip[dst, lines, :] = value

    def step(src, prev, dst, a, b, t, first, count, loop):
        def row(i, state):
            v, fall_above = state
            below = [basis[src, i + 1, j] for j in range(J)]
            fall = [coef[2, i, j] * (v[j] - below[j]) for j in range(J)]
            line = pl.ds(i + (GHOST - D), 1)
            to_left = [rolled(v[j], -1, 1) for j in range(J)]
            beyond = jnp.where(
                sub_id == SUB - 1, jnp.broadcast_to(strip_next[t, line, :], (SUB, LANES)), rolled(to_left[0], -1, 0)
            )
            flow = [
                coef[1, i, j] * (v[j] - jnp.where(lane_id == LANES - 1, to_left[j + 1] if j + 1 < J else beyond, to_left[j]))
                for j in range(J)
            ]
            to_right = [rolled(f, 1, 1) for f in flow]
            before = jnp.where(
                sub_id == 0, jnp.broadcast_to(strip_flow[t, line, :], (SUB, LANES)), rolled(to_right[J - 1], 1, 0)
            )
            for j in range(J):
                arriving = jnp.where(lane_id == 0, to_right[j - 1] if j else before, to_right[j])
                value = (coef[0, i, j] - a) * v[j] + ((flow[j] - arriving) + (fall[j] - fall_above[j]))
                if b is not None:
                    value = value - times(b, basis[prev, i, j])
                basis[dst, i, j] = value
            return below, fall

        v = [basis[src, first, j] for j in range(J)]
        state = v, [coef[2, first - 1, j] * (basis[src, first - 1, j] - v[j]) for j in range(J)]
        if not loop:
            for i in range(first, first + count):
                state = row(i, state)
            return
        unroll = next(u for u in (7, 6, 5, 4, 3, 2, 1) if count % u == 0)

        def body(n, state):
            for m in range(unroll):
                state = row(first + n * unroll + m, state)
            return state

        lax.fori_loop(0, count // unroll, body, state)

    def inner(recurrence, more, again):
        lines = inside if again else everywhere
        for t, (src, prev, dst, a, b) in enumerate(recurrence):
            strip_ready(src, t, lines)
            step(src, prev, dst, a, b, t, D + t + 1, R - 2 - 2 * t, True)
            if more or t + 1 < len(recurrence):
                strip_step(src, prev, dst, a, b, lines)

    def outer(recurrence, more, again):
        depth = len(recurrence)
        for t, (src, prev, dst, a, b) in enumerate(recurrence):
            if again:
                strip_ready(src, t, everywhere)
            step(src, prev, dst, a, b, t, D - (depth - 1 - t), depth, False)
            step(src, prev, dst, a, b, t, D + R - 1 - t, depth, False)
            if again and (more or t + 1 < depth):
                strip_step(src, prev, dst, a, b, everywhere)

    def dots(pairs, base):
        for g in range(0, len(pairs), 8):
            group = pairs[g : g + 8]
            slots = sorted({s for pair in group for s in pair})

            def body(i, sums):
                for j in range(J):
                    held = {s: basis[s, D + i, j] for s in slots}
                    sums = tuple(total + held[p] * held[q] for total, (p, q) in zip(sums, group))
                return sums

            sums = lax.fori_loop(0, R, body, (zero,) * len(group), unroll=2)
            for n, total in enumerate(sums):
                k = base + g + n
                folds[k : k + 1, :] = jnp.sum(total, axis=0, keepdims=True)

    def combine(targets, first, count):
        slots = sorted({s for _, terms in targets for s in terms})

        def body(i, c):
            for j in range(J):
                held = {s: basis[s, first + i, j] for s in slots}
                for target, terms in targets:
                    total = None
                    for s, weight in terms.items():
                        total = added(total, times(weight, held[s]))
                    if callable(target):
                        target(i, j, total)
                    else:
                        basis[target, first + i, j] = total
            return c

        lax.fori_loop(0, count, body, 0)

    def reduce(slot, count):
        n = -(-count // SUB) * SUB
        part = jnp.broadcast_to(jnp.sum(folds[0:n, :], axis=1, keepdims=True), (n, LANES))
        mine = lax.broadcasted_iota(jnp.int32, (n, LANES), 0) == lax.broadcasted_iota(jnp.int32, (n, LANES), 1)
        by_device[slot, me] = jnp.sum(jnp.where(mine, part, 0.0), axis=0, keepdims=True)

        def outgoing(k):
            here = by_device.at[slot, me]
            return pltpu.make_async_remote_copy(
                src_ref=here, dst_ref=here, send_sem=sum_send.at[slot, k], recv_sem=sum_recv.at[slot, me],
                device_id=peer(k), device_id_type=MESH,
            )

        each(1, devices, lambda k: outgoing(k).start())
        reductions.append(outgoing)

        def finish():
            def arrival(k):
                source = lax.rem(me + k, devices)
                here = by_device.at[slot, source]
                pltpu.make_async_remote_copy(
                    src_ref=here, dst_ref=here, send_sem=sum_send.at[slot, k], recv_sem=sum_recv.at[slot, source],
                    device_id=peer(k), device_id_type=MESH,
                ).wait_recv()

            each(1, devices, arrival)
            if devices <= 32:
                parts = [by_device[slot, k] for k in range(devices)]
                while len(parts) > 1:
                    parts = [a + b for a, b in zip(parts[::2], parts[1::2])] + parts[len(parts) // 2 * 2 :]
                total = parts[0]
            else:
                total = lax.fori_loop(1, devices, lambda k, t: t + by_device[slot, k], by_device[slot, 0])
            return [jnp.broadcast_to(total[:, k : k + 1], (SUB, LANES)) for k in range(count)]

        return finish

    v_a = [CENTER] * SWITCH
    v_b = [None, 2.0 * SPREAD] + [SPREAD] * (SWITCH - 1)
    v_b[KNOWN] = None

    opening = send_rows(0, 1, BLOCKS[0]) + send_coefs(0, BLOCKS[0])
    sides = [
        copy(edge_send.at[0], edge_right, lefthand, has_left, has_right),
        copy(edge_send.at[1], edge_left, righthand, has_right, has_left),
    ]
    meet_on()
    inner_coefficients()
    arrive(sides)
    meet_on()
    for band in range(bands):
        own = slice(GHOST + band * SUB, GHOST + (band + 1) * SUB)
        for n in range(4):
            left_border = jnp.where(lane_id < HALF, edge_send[0, band, n], edge_left[band, n])
            right_border = jnp.where(lane_id < HALF, edge_right[band, n], edge_send[1, band, n])
            here = strip_coef.at[n] if n < 3 else strip.at[0]
            at_left = jnp.logical_or(lane_id < HALF // 2, lane_id >= LANES - HALF // 2)
            here[own, :] = jnp.where(at_left, left_border, rolled(right_border, HALF, 1))
    ghosts = send_strips([0]) + [
        copy(strip_coef.at[:, pl.ds(GHOST, GHOST)], strip_coef.at[:, pl.ds(GHOST + R, GHOST)], up, has_above, has_below),
        copy(strip_coef.at[:, pl.ds(R, GHOST)], strip_coef.at[:, pl.ds(0, GHOST)], down, has_below, has_above),
    ]
    deeper = []
    k = 0
    w_a = w_b = None
    one = jnp.ones((SUB, LANES), jnp.float32)
    for n, block in enumerate(BLOCKS):
        slot = (lambda i: i) if k < SWITCH else w_slot
        more = k + block < ITERS
        if k == KNOWN:
            while met[1] is not None:
                meet_on()
            base = starts[n - 1]
            direct = chained(base, KNOWN)
            dots(direct, len(pairs))
            pairs = pairs + direct
            early = reduce(0, len(pairs))
        if n == 0:
            copies = opening + ghosts
        else:
            copies = send_rows(slot(k), 1, block)
            if k == SWITCH:
                copies = copies + send_strips([slot(k)])
            elif k != KNOWN:
                copies = copies + send_rows(slot(k - 1), 2, block - 2)
            if n == 1 and BLOCKS[0] < D:
                deeper = send_coefs(BLOCKS[0], D)
        v_or_w = (v_a, v_b) if k < SWITCH else (w_a, w_b)
        recurrence = [
            (slot(i), slot(i - 1) if i else None, slot(i + 1), v_or_w[0][i], v_or_w[1][i]) for i in range(k, k + block)
        ]
        if k == SWITCH:
            combine(final, D + D, R - 2 * D)
        again = n == 0 or k == SWITCH
        inner(recurrence, more, again)
        if k < KNOWN:
            meet_on()
        if k == SWITCH:
            combine([(w_slot(i), {s: weights[i][s] for s in range(i + 1)}) for i in range(1, SWITCH)], D, R)
            grams = [(i, j) for i in range(SWITCH + 1) for j in range(i + 1)]
            dots([(w_slot(i), w_slot(j)) for i, j in grams], 0)
        elif k > SWITCH:
            added_pairs = chained(starts[n - 1], k)
            dots([(w_slot(i), w_slot(j)) for i, j in added_pairs], len(grams))
            grams = grams + added_pairs
        if not more:
            middle = reduce(1, len(grams))
        if k + block == KNOWN:
            pairs = [(i, j) for i in range(k + 1) for j in range(i + 1)]
            dots(pairs, 0)
        arrive(copies)
        if k < KNOWN:
            meet_on()
        if block > BLOCKS[0] and deeper:
            arrive(deeper)
            deeper = []
        outer(recurrence, more, again)
        k += block
        if k == SWITCH:
            entries = dict(zip(pairs, early()))
            known = Lanczos(v_a)
            for i in range(base + 1, KNOWN + 1):
                fill(entries, i, v_a, v_b)
            for i in range(KNOWN + 1):
                known.row(i, [entries[i, j] for j in range(i + 1)])
            w_a = known.alphas + [known.alphas[-1]] * (ITERS - KNOWN)
            w_b = known.betas + [known.betas[-1]] * (ITERS - KNOWN)
            weights = [[one]]
            for i in range(SWITCH):
                value = applied(weights[i] + [None], v_a + [None], v_b + [None], i + 2)
                value = [minus(p, times(w_a[i], q)) for p, q in zip(value, weights[i] + [None])]
                if i:
                    value = [minus(p, times(w_b[i], q)) for p, q in zip(value, weights[i - 1] + [None] * 2)]
                weights.append(value)
            w_b[SWITCH] = None
            final = [(w_slot(SWITCH), dict(enumerate(weights[SWITCH])))]
            combine(final, D, D)
            combine(final, D + R - D, D)
            for target, terms in final:
                for band in range(bands):
                    own = slice(GHOST + band * SUB, GHOST + (band + 1) * SUB)
                    total = None
                    for s, weight in terms.items():
                        total = added(total, times(weight, strip[s, own, :]))
                    strip[target, own, :] = total

    full = starts[-1]
    direct = chained(full, ITERS)[:-1]
    dots([(w_slot(i), w_slot(j)) for i, j in direct], 0)
    late = reduce(2, len(direct))
    entries = dict(zip(grams, middle()))

    state = Lanczos(w_a)
    x, r, p = [None] * (ITERS + 1), [one], [one]
    pad = [None]
    inverse = None

    def iterate(i):
        nonlocal x, r, p, inverse
        pivot = state.alphas[i] if i == 0 else state.alphas[i] - state.betas[i] * inverse
        inverse = 1.0 / pivot
        image = applied(p + pad, w_a + pad, w_b + pad, i + 2)
        gain = SCALE * inverse
        x = [added(q, times(gain, s)) for q, s in zip(x, p + pad * (ITERS + 1 - len(p)))]
        r = [minus(q, times(inverse, s)) for q, s in zip(r + pad, image)]
        if i + 1 < ITERS:
            ratio = state.betas[i + 1] * inverse * inverse
            p = [added(q, times(ratio, s)) for q, s in zip(r, p + pad)]

    for i in range(full + 1):
        if i > SWITCH:
            fill(entries, i, w_a, w_b)
        state.row(i, [entries[i, j] for j in range(i + 1)])
        if i:
            iterate(i - 1)
    entries.update(zip(direct, late()))
    for i in range(full + 1, ITERS + 1):
        fill(entries, i, w_a, w_b)
        state.row(i, [entries[i, j] for j in range(min(i + 1, ITERS))], i == ITERS)
        iterate(i - 1)

    def store(ref):
        def put(i, j, value):
            band, within = i // SUB, lax.rem(i, SUB)
            ref[pl.ds(band * (tiles * SUB) + j * SUB + within, SUB, stride=J * SUB), :] = value

        return put

    combine(
        [
            (store(x_out), {w_slot(i): x[i] for i in range(ITERS)}),
            (store(r_out), {w_slot(i): r[i] for i in range(ITERS + 1)}),
        ],
        D, R,
    )
    for c, sends in pending:
        pl.when(sends)(c.wait_send)
    for outgoing in reductions:
        each(1, devices, lambda k: outgoing(k).wait_send())


def solution(mesh):
    nr, nc = mesh.shape["rows"], mesh.shape["cols"]

    def on_device(*inputs):
        rows, cols = inputs[0].shape
        bands, tiles, chunk = rows // SUB, cols // LANES, cols // (SUB * LANES)

        def pieces(a):
            return a.reshape(bands, SUB, tiles, LANES).transpose(0, 2, 1, 3).reshape(bands * tiles * SUB, LANES)

        def whole(a):
            return a.reshape(bands, tiles, SUB, LANES).transpose(0, 2, 1, 3).reshape(rows, cols)

        def held(*shape):
            return pltpu.VMEM(shape, jnp.float32)

        block = jax.ShapeDtypeStruct((bands * tiles * SUB, LANES), jnp.float32)
        high, tall = rows + 2 * DEPTH, rows + 2 * GHOST
        slots = SWITCH + ITERS + 1
        dma = pltpu.SemaphoreType.DMA
        both = pl.pallas_call(
            functools.partial(kernel, nr, nc, rows, cols),
            out_shape=pltpu.VMEM((2,) + block.shape, jnp.float32),
            in_specs=[pl.BlockSpec(memory_space=pl.ANY)] * 5,
            out_specs=pl.BlockSpec(memory_space=pltpu.VMEM),
            scratch_shapes=[pltpu.VMEM(block.shape, a.dtype) for a in inputs]
            + [
                held(slots, high, chunk, SUB, LANES),
                held(3, high, chunk, SUB, LANES),
                held(slots, tall, LANES),
                held(3, tall, LANES),
                held(DEPTH, tall, LANES),
                held(DEPTH, tall, LANES),
                held(2, bands, 4, SUB, LANES),
                held(bands, 4, SUB, LANES),
                held(bands, 4, SUB, LANES),
                held(96, LANES),
                held(3, nr * nc, 1, LANES),
                dma((5,)), pltpu.SemaphoreType.REGULAR((MEETINGS,)),
                dma((COPIES,)), dma((COPIES,)), dma((3, nr * nc)), dma((3, nr * nc)),
            ],
            compiler_params=pltpu.CompilerParams(collective_id=0, has_side_effects=True),
        )(*(pieces(a) for a in inputs))
        return whole(both[0]), whole(both[1])

    spec = P("rows", "cols")
    return jax.shard_map(
        on_device, mesh=mesh, in_specs=(spec,) * 5, out_specs=(spec, spec), check_vma=False
    )
```

```python
import functools

import jax
import jax.numpy as jnp
from jax import lax
from jax.experimental import pallas as pl
from jax.experimental.pallas import tpu as pltpu
from jax.sharding import PartitionSpec as P

ITERS = 12

prior_weight = 0.1
smooth_weight = 2.0
LANES = 128
SUB = 8
HALF = LANES // 2
MESH = pl.DeviceIdType.MESH

SCALE = 0.25
CENTER = 9.0 * SCALE
SPREAD = 16.0 * SCALE * SCALE
BLOCKS = (2, 2, 4, 4)
KNOWN = 4
SWITCH = 8
DEPTH = max(BLOCKS)
GHOST = SUB
COPIES = 64
MEETINGS = 16


def each(start, stop, body):
    if stop - start < 32:
        for k in range(start, stop):
            body(k)
    else:
        lax.fori_loop(start, stop, lambda k, c: (body(k), c)[1], 0)


class Lanczos:
    def __init__(self, a):
        self.a, self.lower, self.pivots, self.inverses = a, {}, [], []
        self.alphas, self.betas = [], [None]

    def row(self, k, entries, last=False):
        reduced = []
        for j in range(k):
            value = entries[j]
            for i in range(j):
                value = value - reduced[i] * self.lower[j, i]
            reduced.append(value)
            self.lower[k, j] = value * self.inverses[j]
        if k:
            value = self.a[k - 1] + self.lower[k, k - 1]
            self.alphas.append(value - self.lower[k - 1, k - 2] if k > 1 else value)
        if last:
            return
        pivot = entries[k]
        for i in range(k):
            pivot = pivot - reduced[i] * self.lower[k, i]
        if k:
            self.betas.append(pivot * self.inverses[-1])
        self.pivots.append(pivot)
        self.inverses.append(1.0 / pivot)


def added(x, y):
    return y if x is None else (x if y is None else x + y)


def times(c, x):
    return None if x is None or c is None else (x if isinstance(c, float) and c == 1.0 else c * x)


def minus(x, y):
    return x if y is None else (-y if x is None else x - y)


def chained(full, stop):
    return [(i, j) for i in range(full + 1, stop + 1) for j in (i - 1, i)]


def fill(entries, i, a, b):
    m = i - 1

    def entry(p, q):
        return entries[max(p, q), min(p, q)]

    for j in range(m):
        value = minus(entry(m, j + 1), times(b[m], entry(m - 1, j)))
        if not (isinstance(a[j], float) and a[j] == a[m]):
            value = value + (a[j] - a[m]) * entry(m, j)
        entries[i, j] = added(value, times(b[j], entry(m, j - 1))) if j else value


def applied(p, a, b, size):
    out = [None] * size
    for k, value in enumerate(p):
        if value is None:
            continue
        out[k] = added(out[k], times(a[k], value))
        if k + 1 < size:
            out[k + 1] = added(out[k + 1], value)
        if k:
            out[k - 1] = added(out[k - 1], times(b[k], value))
    return out


def kernel(
    nr, nc, rows, cols,
    depth_in, mask_in, count_in, grad_h_in, grad_v_in,
    both_out,
    depth, hit_mask, hit_count, grad_h, grad_v,
    basis, coef, strip, strip_coef, strip_next, strip_flow,
    edge_send, edge_left, edge_right, folds, by_device,
    load, greet, send, recv, sum_send, sum_recv,
):
    x_out, r_out = both_out.at[0], both_out.at[1]
    me_r = lax.axis_index("rows")
    me_c = lax.axis_index("cols")
    J = cols // (SUB * LANES)
    tiles = cols // LANES
    R, D = rows, DEPTH
    bands = rows // SUB
    tall = rows + 2 * GHOST
    has_above, has_below = me_r > 0, me_r < nr - 1
    has_left, has_right = me_c > 0, me_c < nc - 1
    up, down = (me_r - 1, me_c), (me_r + 1, me_c)
    lefthand, righthand = (me_r, me_c - 1), (me_r, me_c + 1)
    devices = nr * nc
    me = me_r * nc + me_c

    def peer(k):
        other = lax.rem(me + k, devices)
        return (other // nc, lax.rem(other, nc))

    def meet(semaphore, along_rows, along_cols):
        ways = []
        for far, others, me_there, there in (
            (along_rows, nr, me_r, lambda k: (me_r + k, me_c)), (along_cols, nc, me_c, lambda k: (me_r, me_c + k)),
        ):
            if 0 < far < others:
                ways += [(me_there >= far, there(-far)), (me_there < others - far, there(far))]
        for exists, to in ways:
            @pl.when(exists)
            def _():
                pl.semaphore_signal(semaphore, inc=1, device_id=to, device_id_type=MESH)
        count = sum(exists.astype(jnp.int32) for exists, _ in ways)
        return lambda: pl.semaphore_wait(semaphore, count)

    barrier = pltpu.get_barrier_semaphore()
    greeted = meet(barrier, 1, 1)
    loads = [
        pltpu.make_async_copy(a, b, load.at[n])
        for n, (a, b) in enumerate(
            ((grad_h_in, grad_h), (grad_v_in, grad_v), (mask_in, hit_mask), (count_in, hit_count), (depth_in, depth))
        )
    ]
    for c in loads:
        c.start()

    meetings = []
    for axis, others in ((0, nr), (1, nc)):
        far = 1
        while far < others - 1 or (axis and far == 1 and others > 1):
            meetings.append((far, 0) if axis == 0 else (0, far))
            far *= 2
    met = [0, None]

    def meet_on():
        if met[1] is not None:
            met[1]()
            met[1] = None
        if met[0] < len(meetings):
            met[1] = meet(greet.at[met[0]], *meetings[met[0]])
            met[0] += 1

    sub_id = lax.broadcasted_iota(jnp.int32, (SUB, LANES), 0)
    lane_id = lax.broadcasted_iota(jnp.int32, (SUB, LANES), 1)
    zero = jnp.zeros((SUB, LANES), jnp.float32)

    used = [0]
    pending, reductions = [], []

    def copy(src, dst, to, sends, receives):
        k = used[0]
        used[0] += 1
        c = pltpu.make_async_remote_copy(
            src_ref=src, dst_ref=dst, send_sem=send.at[k], recv_sem=recv.at[k], device_id=to, device_id_type=MESH
        )
        pl.when(sends)(c.start)
        pending.append((c, sends))
        return c, receives

    def arrive(copies):
        for c, receives in copies:
            pl.when(receives)(c.wait_recv)

    def local(read, last_col, last_row):
        confidence = (read(hit_mask) * read(hit_count)).astype(jnp.float32) + prior_weight
        h, v = read(grad_h), read(grad_v)
        e = (SCALE * smooth_weight) * jnp.exp(-0.5 * h * h)
        s = (SCALE * smooth_weight) * jnp.exp(-0.5 * v * v)
        if last_col is not None:
            e = jnp.where(jnp.logical_and(last_col, jnp.logical_not(has_right)), 0.0, e)
        if last_row is not None:
            s = jnp.where(jnp.logical_and(last_row, jnp.logical_not(has_below)), 0.0, s)
        return SCALE * confidence, e, s, confidence * read(depth)

    for c in loads:
        c.wait()
    for side in range(2):
        tile = (tiles - 1) * side
        for band in range(bands):
            start = (band * tiles + tile) * SUB
            values = local(
                lambda ref: ref[start : start + SUB, :],
                lane_id == LANES - 1 if side else None,
                sub_id == SUB - 1 if band == bands - 1 else None,
            )
            for n, value in enumerate(values):
                edge_send[side, band, n] = value

    def row_coefficients(r, last_row):
        band, within = r // SUB, lax.rem(r, SUB)
        for j in range(J):
            start = band * (tiles * SUB) + j * SUB + within
            c, e, s, b = local(
                lambda ref: ref[pl.ds(start, SUB, stride=J * SUB), :],
                jnp.logical_and(lane_id == LANES - 1, sub_id == SUB - 1) if j == J - 1 else None,
                sub_id >= 0 if last_row else None,
            )
            coef[0, D + r, j] = c
            coef[1, D + r, j] = e
            coef[2, D + r, j] = s
            basis[0, D + r, j] = b

    def coefficient_rows(start, stop, last=False):
        for r in range(start, stop):
            row_coefficients(r, last and r == R - 1)

    def inner_coefficients():
        pairs = (R - 2 * D) // 2
        lax.fori_loop(0, pairs, lambda i, c: ([row_coefficients(D + 2 * i + t, False) for t in range(2)], c)[1], 0)
        coefficient_rows(D + 2 * pairs, R - D)

    coefficient_rows(0, D)
    coefficient_rows(R - D, R, True)

    def clear_ghost(first, strip_first):
        def _():
            for t in range(D):
                for j in range(J):
                    for n in range(3):
                        coef[n, first + t, j] = zero
                    for slot in exchanged:
                        basis[slot, first + t, j] = zero
            for n in range(3):
                strip_coef[n, strip_first : strip_first + GHOST, :] = zero
            for slot in strips_exchanged:
                strip[slot, strip_first : strip_first + GHOST, :] = zero

        return _

    starts = [sum(BLOCKS[:n]) for n in range(len(BLOCKS))]

    def w_slot(k):
        return SWITCH + k if k else 0

    exchanged = sorted(
        {k if k < SWITCH else w_slot(k) for k in starts}
        | {(k - 1 if k < SWITCH else w_slot(k - 1)) for k in starts if k > 0}
        | set(range(SWITCH))
    )
    strips_exchanged = [0, w_slot(SWITCH)]
    pl.when(jnp.logical_not(has_above))(clear_ghost(0, 0))
    pl.when(jnp.logical_not(has_below))(clear_ghost(D + R, GHOST + R))

    @pl.when(jnp.logical_not(has_left))
    def _():
        edge_left[...] = jnp.zeros_like(edge_left)

    @pl.when(jnp.logical_not(has_right))
    def _():
        edge_right[...] = jnp.zeros_like(edge_right)

    greeted()

    def send_rows(slot, first, count):
        if count <= 0:
            return []
        top = D + first - 1
        bottom = D + R - (first - 1) - count
        return [
            copy(basis.at[slot, pl.ds(top, count)], basis.at[slot, pl.ds(top + R, count)], up, has_above, has_below),
            copy(basis.at[slot, pl.ds(bottom, count)], basis.at[slot, pl.ds(bottom - R, count)], down, has_below, has_above),
        ]

    def send_coefs(old, new):
        copies = []
        count = new - old
        bottom = D + R - new
        copies.append(copy(coef.at[2, pl.ds(bottom, count)], coef.at[2, pl.ds(bottom - R, count)], down, has_below, has_above))
        low, high = max(old, 1), new - 1
        if high >= low:
            n = high - low + 1
            top = D + low - 1
            bottom = D + R - high
            copies.append(copy(coef.at[:, pl.ds(top, n)], coef.at[:, pl.ds(top + R, n)], up, has_above, has_below))
            copies.append(
                copy(coef.at[0:2, pl.ds(bottom, n)], coef.at[0:2, pl.ds(bottom - R, n)], down, has_below, has_above)
            )
        return copies

    def send_strips(slots):
        copies = []
        for slot in slots:
            copies.append(
                copy(
                    strip.at[slot, pl.ds(GHOST, GHOST)], strip.at[slot, pl.ds(GHOST + R, GHOST)],
                    up, has_above, has_below,
                )
            )
            copies.append(
                copy(strip.at[slot, pl.ds(R, GHOST)], strip.at[slot, pl.ds(0, GHOST)], down, has_below, has_above)
            )
        return copies

    def rolled(v, shift, axis):
        return pltpu.roll(v, shift % v.shape[axis], axis)

    everywhere, inside = slice(0, tall), slice(GHOST, GHOST + R)

    def strip_ready(src, t, lines):
        v = strip[src, lines, :]
        strip_flow[t, lines, :] = rolled(strip_coef[1, lines, :] * (v - rolled(v, -1, 1)), 1, 1)
        strip_next[t, lines, :] = rolled(v, HALF - 1, 1)

    def strip_step(src, prev, dst, a, b, lines):
        def spread(c):
            return c if isinstance(c, float) else jnp.concatenate([c] * ((lines.stop - lines.start) // SUB), axis=0)

        v = strip[src, lines, :]
        flow = strip_coef[1, lines, :] * (v - rolled(v, -1, 1))
        fall = strip_coef[2, lines, :] * (v - rolled(v, -1, 0))
        value = (strip_coef[0, lines, :] - spread(a)) * v
        value = value + (flow - rolled(flow, 1, 1)) + (fall - rolled(fall, 1, 0))
        if b is not None:
            value = value - times(spread(b), strip[prev, lines, :])
        strip[dst, lines, :] = value

    def step(src, prev, dst, a, b, t, first, count, loop):
        def row(i, state):
            v, fall_above = state
            below = [basis[src, i + 1, j] for j in range(J)]
            fall = [coef[2, i, j] * (v[j] - below[j]) for j in range(J)]
            line = pl.ds(i + (GHOST - D), 1)
            to_left = [rolled(v[j], -1, 1) for j in range(J)]
            beyond = jnp.where(
                sub_id == SUB - 1, jnp.broadcast_to(strip_next[t, line, :], (SUB, LANES)), rolled(to_left[0], -1, 0)
            )
            flow = [
                coef[1, i, j] * (v[j] - jnp.where(lane_id == LANES - 1, to_left[j + 1] if j + 1 < J else beyond, to_left[j]))
                for j in range(J)
            ]
            to_right = [rolled(f, 1, 1) for f in flow]
            before = jnp.where(
                sub_id == 0, jnp.broadcast_to(strip_flow[t, line, :], (SUB, LANES)), rolled(to_right[J - 1], 1, 0)
            )
            for j in range(J):
                arriving = jnp.where(lane_id == 0, to_right[j - 1] if j else before, to_right[j])
                value = (coef[0, i, j] - a) * v[j] + ((flow[j] - arriving) + (fall[j] - fall_above[j]))
                if b is not None:
                    value = value - times(b, basis[prev, i, j])
                basis[dst, i, j] = value
            return below, fall

        v = [basis[src, first, j] for j in range(J)]
        state = v, [coef[2, first - 1, j] * (basis[src, first - 1, j] - v[j]) for j in range(J)]
        if not loop:
            for i in range(first, first + count):
                state = row(i, state)
            return
        unroll = next(u for u in (7, 6, 5, 4, 3, 2, 1) if count % u == 0)

        def body(n, state):
            for m in range(unroll):
                state = row(first + n * unroll + m, state)
            return state

        lax.fori_loop(0, count // unroll, body, state)

    def inner(recurrence, more, again):
        lines = inside if again else everywhere
        for t, (src, prev, dst, a, b) in enumerate(recurrence):
            strip_ready(src, t, lines)
            step(src, prev, dst, a, b, t, D + t + 1, R - 2 - 2 * t, True)
            if more or t + 1 < len(recurrence):
                strip_step(src, prev, dst, a, b, lines)

    def outer(recurrence, more, again):
        depth = len(recurrence)
        for t, (src, prev, dst, a, b) in enumerate(recurrence):
            if again:
                strip_ready(src, t, everywhere)
            step(src, prev, dst, a, b, t, D - (depth - 1 - t), depth, False)
            step(src, prev, dst, a, b, t, D + R - 1 - t, depth, False)
            if again and (more or t + 1 < depth):
                strip_step(src, prev, dst, a, b, everywhere)

    def dots(pairs, base):
        for g in range(0, len(pairs), 8):
            group = pairs[g : g + 8]
            slots = sorted({s for pair in group for s in pair})

            def body(i, sums):
                for j in range(J):
                    held = {s: basis[s, D + i, j] for s in slots}
                    sums = tuple(total + held[p] * held[q] for total, (p, q) in zip(sums, group))
                return sums

            sums = lax.fori_loop(0, R, body, (zero,) * len(group), unroll=2)
            for n, total in enumerate(sums):
                k = base + g + n
                folds[k : k + 1, :] = jnp.sum(total, axis=0, keepdims=True)

    def combine(targets, first, count):
        slots = sorted({s for _, terms in targets for s in terms})

        def body(i, c):
            for j in range(J):
                held = {s: basis[s, first + i, j] for s in slots}
                for target, terms in targets:
                    total = None
                    for s, weight in terms.items():
                        total = added(total, times(weight, held[s]))
                    if callable(target):
                        target(i, j, total)
                    else:
                        basis[target, first + i, j] = total
            return c

        lax.fori_loop(0, count, body, 0)

    def reduce(slot, count):
        n = -(-count // SUB) * SUB
        part = jnp.broadcast_to(jnp.sum(folds[0:n, :], axis=1, keepdims=True), (n, LANES))
        mine = lax.broadcasted_iota(jnp.int32, (n, LANES), 0) == lax.broadcasted_iota(jnp.int32, (n, LANES), 1)
        by_device[slot, me] = jnp.sum(jnp.where(mine, part, 0.0), axis=0, keepdims=True)

        def outgoing(k):
            here = by_device.at[slot, me]
            return pltpu.make_async_remote_copy(
                src_ref=here, dst_ref=here, send_sem=sum_send.at[slot, k], recv_sem=sum_recv.at[slot, me],
                device_id=peer(k), device_id_type=MESH,
            )

        each(1, devices, lambda k: outgoing(k).start())
        reductions.append(outgoing)

        def finish():
            def arrival(k):
                source = lax.rem(me + k, devices)
                here = by_device.at[slot, source]
                pltpu.make_async_remote_copy(
                    src_ref=here, dst_ref=here, send_sem=sum_send.at[slot, k], recv_sem=sum_recv.at[slot, source],
                    device_id=peer(k), device_id_type=MESH,
                ).wait_recv()

            each(1, devices, arrival)
            if devices <= 32:
                parts = [by_device[slot, k] for k in range(devices)]
                while len(parts) > 1:
                    parts = [a + b for a, b in zip(parts[::2], parts[1::2])] + parts[len(parts) // 2 * 2 :]
                total = parts[0]
            else:
                total = lax.fori_loop(1, devices, lambda k, t: t + by_device[slot, k], by_device[slot, 0])
            return [jnp.broadcast_to(total[:, k : k + 1], (SUB, LANES)) for k in range(count)]

        return finish

    v_a = [CENTER] * SWITCH
    v_b = [None, 2.0 * SPREAD] + [SPREAD] * (SWITCH - 1)
    v_b[KNOWN] = None

    opening = send_rows(0, 1, BLOCKS[0]) + send_coefs(0, BLOCKS[0])
    sides = [
        copy(edge_send.at[0], edge_right, lefthand, has_left, has_right),
        copy(edge_send.at[1], edge_left, righthand, has_right, has_left),
    ]
    meet_on()
    inner_coefficients()
    arrive(sides)
    meet_on()
    for band in range(bands):
        own = slice(GHOST + band * SUB, GHOST + (band + 1) * SUB)
        for n in range(4):
            left_border = jnp.where(lane_id < HALF, edge_send[0, band, n], edge_left[band, n])
            right_border = jnp.where(lane_id < HALF, edge_right[band, n], edge_send[1, band, n])
            here = strip_coef.at[n] if n < 3 else strip.at[0]
            at_left = jnp.logical_or(lane_id < HALF // 2, lane_id >= LANES - HALF // 2)
            here[own, :] = jnp.where(at_left, left_border, rolled(right_border, HALF, 1))
    ghosts = send_strips([0]) + [
        copy(strip_coef.at[:, pl.ds(GHOST, GHOST)], strip_coef.at[:, pl.ds(GHOST + R, GHOST)], up, has_above, has_below),
        copy(strip_coef.at[:, pl.ds(R, GHOST)], strip_coef.at[:, pl.ds(0, GHOST)], down, has_below, has_above),
    ]
    deeper = []
    k = 0
    w_a = w_b = None
    one = jnp.ones((SUB, LANES), jnp.float32)
    for n, block in enumerate(BLOCKS):
        slot = (lambda i: i) if k < SWITCH else w_slot
        more = k + block < ITERS
        if k == KNOWN:
            while met[1] is not None:
                meet_on()
            base = starts[n - 1]
            direct = chained(base, KNOWN)
            dots(direct, len(pairs))
            pairs = pairs + direct
            early = reduce(0, len(pairs))
        if n == 0:
            copies = opening + ghosts
        else:
            copies = send_rows(slot(k), 1, block)
            if k == SWITCH:
                copies = copies + send_strips([slot(k)])
            elif k != KNOWN:
                copies = copies + send_rows(slot(k - 1), 2, block - 2)
            if n == 1 and BLOCKS[0] < D:
                deeper = send_coefs(BLOCKS[0], D)
        v_or_w = (v_a, v_b) if k < SWITCH else (w_a, w_b)
        recurrence = [
            (slot(i), slot(i - 1) if i else None, slot(i + 1), v_or_w[0][i], v_or_w[1][i]) for i in range(k, k + block)
        ]
        if k == SWITCH:
            combine(final, D + D, R - 2 * D)
        again = n == 0 or k == SWITCH
        inner(recurrence, more, again)
        if k < KNOWN:
            meet_on()
        if k == SWITCH:
            combine([(w_slot(i), {s: weights[i][s] for s in range(i + 1)}) for i in range(1, SWITCH)], D, R)
            grams = [(i, j) for i in range(SWITCH + 1) for j in range(i + 1)]
            dots([(w_slot(i), w_slot(j)) for i, j in grams], 0)
        elif k > SWITCH:
            added_pairs = chained(starts[n - 1], k)
            dots([(w_slot(i), w_slot(j)) for i, j in added_pairs], len(grams))
            grams = grams + added_pairs
        if not more:
            middle = reduce(1, len(grams))
        if k + block == KNOWN:
            pairs = [(i, j) for i in range(k + 1) for j in range(i + 1)]
            dots(pairs, 0)
        arrive(copies)
        if k < KNOWN:
            meet_on()
        if block > BLOCKS[0] and deeper:
            arrive(deeper)
            deeper = []
        outer(recurrence, more, again)
        k += block
        if k == SWITCH:
            entries = dict(zip(pairs, early()))
            known = Lanczos(v_a)
            for i in range(base + 1, KNOWN + 1):
                fill(entries, i, v_a, v_b)
            for i in range(KNOWN + 1):
                known.row(i, [entries[i, j] for j in range(i + 1)])
            w_a = known.alphas + [known.alphas[-1]] * (ITERS - KNOWN)
            w_b = known.betas + [known.betas[-1]] * (ITERS - KNOWN)
            weights = [[one]]
            for i in range(SWITCH):
                value = applied(weights[i] + [None], v_a + [None], v_b + [None], i + 2)
                value = [minus(p, times(w_a[i], q)) for p, q in zip(value, weights[i] + [None])]
                if i:
                    value = [minus(p, times(w_b[i], q)) for p, q in zip(value, weights[i - 1] + [None] * 2)]
                weights.append(value)
            w_b[SWITCH] = None
            final = [(w_slot(SWITCH), dict(enumerate(weights[SWITCH])))]
            combine(final, D, D)
            combine(final, D + R - D, D)
            for target, terms in final:
                for band in range(bands):
                    own = slice(GHOST + band * SUB, GHOST + (band + 1) * SUB)
                    total = None
                    for s, weight in terms.items():
                        total = added(total, times(weight, strip[s, own, :]))
                    strip[target, own, :] = total

    full = starts[-1]
    direct = chained(full, ITERS)[:-1]
    dots([(w_slot(i), w_slot(j)) for i, j in direct], 0)
    late = reduce(2, len(direct))
    entries = dict(zip(grams, middle()))

    state = Lanczos(w_a)
    x, r, p = [None] * (ITERS + 1), [one], [one]
    pad = [None]
    inverse = None

    def iterate(i):
        nonlocal x, r, p, inverse
        pivot = state.alphas[i] if i == 0 else state.alphas[i] - state.betas[i] * inverse
        inverse = 1.0 / pivot
        image = applied(p + pad, w_a + pad, w_b + pad, i + 2)
        gain = SCALE * inverse
        x = [added(q, times(gain, s)) for q, s in zip(x, p + pad * (ITERS + 1 - len(p)))]
        r = [minus(q, times(inverse, s)) for q, s in zip(r + pad, image)]
        if i + 1 < ITERS:
            ratio = state.betas[i + 1] * inverse * inverse
            p = [added(q, times(ratio, s)) for q, s in zip(r, p + pad)]

    for i in range(full + 1):
        if i > SWITCH:
            fill(entries, i, w_a, w_b)
        state.row(i, [entries[i, j] for j in range(i + 1)])
        if i:
            iterate(i - 1)
    entries.update(zip(direct, late()))
    for i in range(full + 1, ITERS + 1):
        fill(entries, i, w_a, w_b)
        state.row(i, [entries[i, j] for j in range(min(i + 1, ITERS))], i == ITERS)
        iterate(i - 1)

    def store(ref):
        def put(i, j, value):
            band, within = i // SUB, lax.rem(i, SUB)
            ref[pl.ds(band * (tiles * SUB) + j * SUB + within, SUB, stride=J * SUB), :] = value

        return put

    combine(
        [
            (store(x_out), {w_slot(i): x[i] for i in range(ITERS)}),
            (store(r_out), {w_slot(i): r[i] for i in range(ITERS + 1)}),
        ],
        D, R,
    )
    for c, sends in pending:
        pl.when(sends)(c.wait_send)
    for outgoing in reductions:
        each(1, devices, lambda k: outgoing(k).wait_send())


def solution(mesh):
    nr, nc = mesh.shape["rows"], mesh.shape["cols"]

    def on_device(*inputs):
        rows, cols = inputs[0].shape
        bands, tiles, chunk = rows // SUB, cols // LANES, cols // (SUB * LANES)

        def pieces(a):
            return a.reshape(bands, SUB, tiles, LANES).transpose(0, 2, 1, 3).reshape(bands * tiles * SUB, LANES)

        def whole(a):
            return a.reshape(bands, tiles, SUB, LANES).transpose(0, 2, 1, 3).reshape(rows, cols)

        def held(*shape):
            return pltpu.VMEM(shape, jnp.float32)

        block = jax.ShapeDtypeStruct((bands * tiles * SUB, LANES), jnp.float32)
        high, tall = rows + 2 * DEPTH, rows + 2 * GHOST
        slots = SWITCH + ITERS + 1
        dma = pltpu.SemaphoreType.DMA
        both = pl.pallas_call(
            functools.partial(kernel, nr, nc, rows, cols),
            out_shape=pltpu.VMEM((2,) + block.shape, jnp.float32),
            in_specs=[pl.BlockSpec(memory_space=pl.ANY)] * 5,
            out_specs=pl.BlockSpec(memory_space=pltpu.VMEM),
            scratch_shapes=[pltpu.VMEM(block.shape, a.dtype) for a in inputs]
            + [
                held(slots, high, chunk, SUB, LANES),
                held(3, high, chunk, SUB, LANES),
                held(slots, tall, LANES),
                held(3, tall, LANES),
                held(DEPTH, tall, LANES),
                held(DEPTH, tall, LANES),
                held(2, bands, 4, SUB, LANES),
                held(bands, 4, SUB, LANES),
                held(bands, 4, SUB, LANES),
                held(96, LANES),
                held(3, nr * nc, 1, LANES),
                dma((5,)), pltpu.SemaphoreType.REGULAR((MEETINGS,)),
                dma((COPIES,)), dma((COPIES,)), dma((3, nr * nc)), dma((3, nr * nc)),
            ],
            compiler_params=pltpu.CompilerParams(collective_id=0, has_side_effects=True),
        )(*(pieces(a) for a in inputs))
        return whole(both[0]), whole(both[1])

    spec = P("rows", "cols")
    return jax.shard_map(
        on_device, mesh=mesh, in_specs=(spec,) * 5, out_specs=(spec, spec), check_vma=False
    )
```
